256 devices in a mesh: gz: 32 (over x_hi, z, core), gy: 8 (over x_lo, y).
Axes of the slice: x: 4 (x_hi: 2, x_lo: 2; x = x_hi * 2 + x_lo), y: 4, z: 8, core: 2. Of those that a mesh axis runs over, the one named last changes fastest.
Arguments:
- level_set: float32 [512, 256, 256], P('gz', 'gy'), may hold values from -8 to 8
Outputs:
- reinitialized: float32 [512, 256, 256], P('gz', 'gy')
The draws below stay inside these ranges and needn't reach their ends.
All inputs are finite; a program needn't handle non-finite values.
Results may differ from the reference program's by a relative error of at most 0.0003.
Values sent between devices are 32-bit elements; how exact they have to be, the bound alone decides.
No kernel may reach another device: no remote copies, remote signals or barrier semaphores. Data moves between devices by JAX's collectives and lax.ppermute only.
A program may use at most 64 MiB of HBM per device.

```python
import jax
import jax.numpy as jnp
from jax import lax

CZ = 16
NX = 256
STEPS = 2
NZ = 512
NY = 256
N_GZ = 32


def block_levels(stream_key, shape, shards, least, top_value):
    factor_of = 1.0
    for position, blocks in shards:
        steps = jax.random.uniform(jax.random.fold_in(jax.random.fold_in(stream_key, 6), position), (blocks,), jnp.float32, least / len(shards), top_value / len(shards))
        factor_of = factor_of * jnp.repeat(jnp.exp(steps), shape[position] // blocks).reshape((-1,) + (1,) * (len(shape) - 1 - position))
    return factor_of


def centred(stream_key, shape, scale, bound, split=(), kind=jnp.bfloat16):
    entries = jax.random.normal(stream_key, shape, jnp.float32) * scale
    if len(split) > 0:
        entries = block_levels(stream_key, shape, split, -0.22, 0.18) * entries
    return jnp.clip(entries, min=-bound, max=bound).astype(kind)


def setup_inputs(seed: int = 0) -> dict:
    key_list = jax.random.split(jax.random.key(seed), 2)
    return {
        "level_set": centred(key_list[0], (NZ, NY, NX), 2.0, 8.0, ((0, 32), (1, 8)), jnp.float32),
    }


weno_eps = 1e-06
pseudo_step = 0.3

def weno_five(first, second, third, fourth, fifth):
    cand_one = first / 3.0 - 7.0 * second / 6.0 + 11.0 * third / 6.0
    cand_two = -second / 6.0 + 5.0 * third / 6.0 + fourth / 3.0
    cand_three = third / 3.0 + 5.0 * fourth / 6.0 - fifth / 6.0
    smooth_one = 13.0 / 12.0 * (first - 2.0 * second + third) ** 2 + 0.25 * (first - 4.0 * second + 3.0 * third) ** 2
    smooth_two = 13.0 / 12.0 * (second - 2.0 * third + fourth) ** 2 + 0.25 * (second - fourth) ** 2
    smooth_three = 13.0 / 12.0 * (third - 2.0 * fourth + fifth) ** 2 + 0.25 * (3.0 * third - 4.0 * fourth + fifth) ** 2
    alpha_one = 0.1 / (weno_eps + smooth_one) ** 2
    alpha_two = 0.6 / (weno_eps + smooth_two) ** 2
    alpha_three = 0.3 / (weno_eps + smooth_three) ** 2
    total = alpha_one + alpha_two + alpha_three
    return (alpha_one * cand_one + alpha_two * cand_two + alpha_three * cand_three) / total

def weno_pair(padded, axis):
    length = padded.shape[axis] - 6
    diffs = jnp.diff(padded, axis=axis)
    parts = [lax.slice_in_dim(diffs, k, k + length, axis=axis) for k in range(6)]
    backward = weno_five(parts[0], parts[1], parts[2], parts[3], parts[4])
    forward = weno_five(parts[5], parts[4], parts[3], parts[2], parts[1])
    return (backward, forward)

def godunov(backward, forward, positive):
    plus_case = jnp.maximum(jnp.maximum(backward, 0.0) ** 2, jnp.minimum(forward, 0.0) ** 2)
    minus_case = jnp.maximum(jnp.minimum(backward, 0.0) ** 2, jnp.maximum(forward, 0.0) ** 2)
    return jnp.where(positive, plus_case, minus_case)

def rate(z_ext, y_ext, center, sign):
    positive = sign >= 0.0
    back_z, fore_z = weno_pair(z_ext, 0)
    back_y, fore_y = weno_pair(y_ext, 1)
    x_ext = jnp.pad(center, ((0, 0), (0, 0), (3, 3)), mode='edge')
    back_x, fore_x = weno_pair(x_ext, 2)
    squared = godunov(back_z, fore_z, positive) + godunov(back_y, fore_y, positive) + godunov(back_x, fore_x, positive)
    return -sign * (jnp.sqrt(squared) - 1.0)

def global_rate(field, sign):
    z_pad = jnp.concatenate([field[-3:], field, field[:3]], axis=0)
    y_pad = jnp.pad(field, ((0, 0), (3, 3), (0, 0)), mode='edge')

    def one_block(index):
        start = index * CZ
        z_ext = lax.dynamic_slice_in_dim(z_pad, start, CZ + 6, 0)
        y_ext = lax.dynamic_slice_in_dim(y_pad, start, CZ, 0)
        center = lax.dynamic_slice_in_dim(field, start, CZ, 0)
        local_sign = lax.dynamic_slice_in_dim(sign, start, CZ, 0)
        return rate(z_ext, y_ext, center, local_sign)
    blocks = lax.map(one_block, jnp.arange(N_GZ, dtype=jnp.int32))
    return blocks.reshape(field.shape)

def reference(level_set):
    sign = level_set / jnp.sqrt(level_set * level_set + 1.0)
    field = level_set
    for step in range(STEPS):
        first = field + pseudo_step * global_rate(field, sign)
        second = 0.75 * field + 0.25 * (first + pseudo_step * global_rate(first, sign))
        field = 1.0 / 3.0 * field + 2.0 / 3.0 * (second + pseudo_step * global_rate(second, sign))
    return field
```

```python
import functools

import jax
import jax.numpy as jnp
from jax import lax
from jax.experimental import pallas as pl
from jax.experimental.pallas import tpu as pltpu
from jax.sharding import PartitionSpec as P

STEPS = 2
TAU = 0.3
EPS = 0.75e-6

DEEP = 9
PITCH = 64
ROW0 = 16
f32 = jnp.float32


def triple(g, h, curve):
    lean = 1.5 * curve
    mid = curve * curve + (0.75 * (g * h) + EPS)
    left = mid + lean * h
    right = mid - lean * g
    return left * left, mid * mid, right * right


def face(a, b, c, jump_low, jump_high, base_back, base_fore):
    p = b * c
    q = a * c
    r = a * b
    half = 0.5 * (p + r) + 3.0 * q
    pj = p * jump_low
    rj = r * jump_high
    back = base_back - (pj + 1.5 * rj) / (half + r)
    fore = base_fore - (1.5 * pj + rj) / (half + p)
    return back, fore


def upwind(back, fore, side):
    best = jnp.maximum(jnp.maximum(side * back, side * fore), 0.0)
    return best * best


def bases(center, low_slope, high_slope):
    six = 6.0 * center
    both = low_slope + high_slope
    return six + (both + high_slope), (both + low_slope) - six


def at(z, r, n=8):
    return pl.ds(z * PITCH + r, n)


def z_pass(src, side, acc, margin, tiles):
    first = DEEP - margin
    last = DEEP + 16 + margin
    r0 = ROW0 - margin

    def column(t, carry):
        r = r0 + 8 * t
        state = [dict(), dict()]
        for k in range(first - 1, last):
            for h in range(2):
                s = state[h]

                def u(z):
                    if ("u", z) not in s:
                        s["u", z] = src[h, at(z, r), :]
                    return s["u", z]

                def d(z):
                    if ("d", z) not in s:
                        s["d", z] = u(z + 1) - u(z)
                    return s["d", z]

                def e(z):
                    if ("e", z) not in s:
                        s["e", z] = d(z + 1) - d(z)
                    return s["e", z]

                def c(z):
                    if ("c", z) not in s:
                        s["c", z] = e(z) - e(z - 1)
                    return s["c", z]

                def j(z):
                    if ("j", z) not in s:
                        s["j", z] = c(z) - c(z - 1)
                    return s["j", z]

                def tr(z):
                    if ("t", z) not in s:
                        s["t", z] = triple(e(z - 1), e(z), c(z))
                    return s["t", z]

                base_back, base_fore = bases(d(k), e(k - 1), e(k))
                back, fore = face(
                    tr(k - 1)[0], tr(k)[1], tr(k + 1)[2], j(k), j(k + 1), base_back, base_fore
                )
                if k >= first:
                    acc[h, pl.ds((k - first) * 48 + 8 * t, 8), :] = upwind(
                        s["back"], fore, side[h, at(k, r), :]
                    )
                s["back"] = back
        return carry

    lax.fori_loop(0, tiles, column, 0)


def y_pass(src, side, acc, scr, margin, tiles, face_tiles, triple_tiles, planes_at_once):
    first = DEEP - margin
    count = 16 + 2 * margin
    r0 = ROW0 - margin
    left_s, mid_s, right_s, curve_s, diff_s, fore_s = scr

    def plane(i, carry):
        for sub in range(planes_at_once):
            zi = i * planes_at_once + sub
            z = first + zi
            for h in range(2):
                slot = sub * 2 + h
                for t in range(triple_tiles):
                    r = r0 - 2 + 8 * t
                    u0 = src[h, at(z, r - 1), :]
                    u1 = src[h, at(z, r), :]
                    u2 = src[h, at(z, r + 1), :]
                    u3 = src[h, at(z, r + 2), :]
                    d1 = u2 - u1
                    g = d1 - (u1 - u0)
                    e = (u3 - u2) - d1
                    curve = e - g
                    rows = pl.ds(8 * t, 8)
                    left_s[slot, rows, :], mid_s[slot, rows, :], right_s[slot, rows, :] = triple(g, e, curve)
                    curve_s[slot, rows, :] = curve
                    diff_s[slot, rows, :] = d1
            for h in range(2):
                slot = sub * 2 + h
                backs = []
                for t in range(face_tiles):
                    lo, me, hi = pl.ds(8 * t, 8), pl.ds(8 * t + 1, 8), pl.ds(8 * t + 2, 8)
                    dl, dm, dh = diff_s[slot, lo, :], diff_s[slot, me, :], diff_s[slot, hi, :]
                    cm = curve_s[slot, me, :]
                    back, fore = face(
                        left_s[slot, lo, :],
                        mid_s[slot, me, :],
                        right_s[slot, hi, :],
                        cm - curve_s[slot, lo, :],
                        curve_s[slot, hi, :] - cm,
                        5.0 * dm + ((dh + dh) - dl),
                        (dh - (dl + dl)) - 5.0 * dm,
                    )
                    fore_s[slot, pl.ds(8 * t, 8), :] = fore
                    backs.append(back)
                for t in range(tiles):
                    fore = fore_s[slot, pl.ds(8 * t + 1, 8), :]
                    rows = pl.ds(zi * 48 + 8 * t, 8)
                    acc[h, rows, :] += upwind(backs[t], fore, side[h, at(z, r0 + 8 * t), :])
        return carry

    lax.fori_loop(0, count // planes_at_once, plane, 0)


def x_pass(src, side, rate_of, acc, put, scr, margin, tiles, combine):
    first = DEEP - margin
    count = 16 + 2 * margin
    r0 = ROW0 - margin
    lane = lax.broadcasted_iota(jnp.int32, (8, 128), 1)
    below_last = lane < 127
    below_two = lane < 126
    above_first = lane > 0
    shifted, finished = (scr[0], scr[1]), (scr[2], scr[3])

    def shift(z, out):
        for t in range(tiles):
            even, odd = src[0, at(z, r0 + 8 * t), :], src[1, at(z, r0 + 8 * t), :]
            rows = pl.ds(8 * t, 8)
            out[0, rows, :] = jnp.where(above_first, pltpu.roll(even, 1, 1), even)
            out[1, rows, :] = jnp.where(above_first, pltpu.roll(odd, 1, 1), even)
            out[2, rows, :] = jnp.where(below_last, pltpu.roll(even, 127, 1), odd)
            odd_up = jnp.where(below_last, pltpu.roll(odd, 127, 1), odd)
            out[3, rows, :] = odd_up
            out[4, rows, :] = jnp.where(below_two, pltpu.roll(even, 126, 1), odd_up)

    def finish(h, zi, t, back, fore):
        z = first + zi
        r = r0 + 8 * t
        total = acc[h, pl.ds(zi * 48 + 8 * t, 8), :] + upwind(back, fore, side[h, at(z, r), :])
        norm = total * lax.rsqrt(jnp.maximum(total, 1e-30))
        stepped = src[h, at(z, r), :] + rate_of[h, at(z, r), :] * ((1.0 / 6.0) * norm - 1.0)
        put(h, zi, t, r, combine(h, z, r, stepped))

    def finish_even(zi, done):
        for t in range(tiles):
            rows = pl.ds(8 * t, 8)
            finish(0, zi, t, done[0, rows, :], done[1, rows, :])

    def faces(zi, inp, done):
        z = first + zi
        for t in range(tiles):
            rows = pl.ds(8 * t, 8)
            u = [
                inp[0, rows, :],
                inp[1, rows, :],
                src[0, at(z, r0 + 8 * t), :],
                src[1, at(z, r0 + 8 * t), :],
                inp[2, rows, :],
                inp[3, rows, :],
                inp[4, rows, :],
            ]
            d = [u[i + 1] - u[i] for i in range(6)]
            e = [d[i + 1] - d[i] for i in range(5)]
            c = [e[i + 1] - e[i] for i in range(4)]
            jump = [c[i + 1] - c[i] for i in range(3)]
            tri = [triple(e[i], e[i + 1], c[i]) for i in range(4)]
            back_even, fore_even = face(
                tri[0][0], tri[1][1], tri[2][2], jump[0], jump[1], *bases(d[2], e[1], e[2])
            )
            back_odd, fore_odd = face(
                tri[1][0], tri[2][1], tri[3][2], jump[1], jump[2], *bases(d[3], e[2], e[3])
            )
            edge, _ = face(EPS * EPS, tri[0][1], tri[1][2], c[0], jump[0], e[1] + e[1], e[1])
            done[0, rows, :] = jnp.where(above_first, pltpu.roll(back_odd, 1, 1), edge)
            done[1, rows, :] = fore_even
            finish(1, zi, t, back_even, fore_odd)

    shift(first, shifted[0])

    def two_planes(i, carry):
        zi = 2 * i
        shift(first + zi + 1, shifted[1])
        finish_even(jnp.maximum(zi - 1, 0), finished[1])
        faces(zi, shifted[0], finished[0])
        shift(first + zi + 2, shifted[0])
        finish_even(zi, finished[0])
        faces(zi + 1, shifted[1], finished[1])
        return carry

    lax.fori_loop(0, count // 2, two_planes, 0)
    finish_even(count - 1, finished[1])


def load_block(work, own_ref, zo_ref, ze_ref, yo_ref, ye_ref, odd_z, odd_y, is_first, is_last):
    def planes(ref, start, count):
        def one(k, carry):
            for t in range(4):
                for h in range(2):
                    work[h, at(start + k, ROW0 + 8 * t), :] = ref[k, h, 8 * t : 8 * t + 8, :]
            return carry

        lax.fori_loop(0, count, one, 0)

    planes(own_ref, DEEP, 16)
    planes(zo_ref, 25 * odd_z, DEEP)
    planes(ze_ref, 25 * (1 - odd_z), DEEP)

    def low(ref):
        def one(z, carry):
            for h in range(2):
                work[h, at(z, ROW0 - 8), :] = ref[h, pl.ds(8 * z, 8), :]
                work[h, at(z, ROW0 - 9, 1), :] = ref[h, pl.ds(272 + z, 1), :]
            return carry

        lax.fori_loop(0, 34, one, 0)

    def high(ref):
        def one(z, carry):
            for h in range(2):
                work[h, at(z, ROW0 + 32), :] = ref[h, pl.ds(8 * z, 8), :]
                work[h, at(z, ROW0 + 40, 1), :] = ref[h, pl.ds(272 + z, 1), :]
            return carry

        lax.fori_loop(0, 34, one, 0)

    @pl.when(odd_y == 0)
    def _():
        low(yo_ref)
        high(ye_ref)

    @pl.when(odd_y == 1)
    def _():
        low(ye_ref)
        high(yo_ref)

    edge_rows(work, 0, 34, True, is_first, is_last)


def edge_rows(work, start, count, far, is_first, is_last):
    @pl.when(is_first)
    def _():
        def one(k, carry):
            z = start + k
            for h in range(2):
                row = work[h, at(z, ROW0, 1), :]
                work[h, at(z, ROW0 - 8), :] = jnp.broadcast_to(row, (8, 128))
                if far:
                    work[h, at(z, ROW0 - 9, 1), :] = row
            return carry

        lax.fori_loop(0, count, one, 0)

    @pl.when(is_last)
    def _():
        def one(k, carry):
            z = start + k
            for h in range(2):
                row = work[h, at(z, ROW0 + 31, 1), :]
                work[h, at(z, ROW0 + 32), :] = jnp.broadcast_to(row, (8, 128))
                if far:
                    work[h, at(z, ROW0 + 40, 1), :] = row
            return carry

        lax.fori_loop(0, count, one, 0)


def step_kernel(initial, *refs):
    refs = list(refs)
    own_ref, zo_ref, ze_ref, yo_ref, ye_ref = refs[:5]
    refs = refs[5:]
    if initial:
        out_ref, so_ref, se_ref, keep = refs[:4]
        refs = refs[4:]
        weight = keep
    else:
        weight, out_ref = refs[:2]
        refs = refs[2:]
    u, first, second, side, acc = refs[:5]
    scr = refs[5:11]
    x_scr = refs[11:15]
    third = refs[15]
    gz, gy = lax.axis_index("gz"), lax.axis_index("gy")
    odd_z, odd_y = lax.rem(gz, 2), lax.rem(gy, 2)
    is_first, is_last = gy == 0, gy == lax.axis_size("gy") - 1
    load_block(u, own_ref, zo_ref, ze_ref, yo_ref, ye_ref, odd_z, odd_y, is_first, is_last)

    def signs(k, carry):
        z = 3 + k
        for h in range(2):
            for t in range(6):
                rows = at(z, 10 + 8 * t)
                if initial:
                    v = u[h, rows, :]
                    w = (-TAU) * (v / jnp.sqrt(v * v + 1.0))
                    weight[h, rows, :] = w
                else:
                    w = weight[h, rows, :]
                side[h, rows, :] = jnp.where(w <= 0.0, 1.0, -1.0)
        return carry

    lax.fori_loop(0, 28, signs, 0)

    def store(work, start):
        def put(h, zi, t, r, value):
            work[h, at(start + zi, r), :] = value

        return put

    def put_out(h, zi, t, r, value):
        out_ref[zi, h, 8 * t : 8 * t + 8, :] = value

    def put_third(h, zi, t, r, value):
        third[h, pl.ds(zi * 32 + 8 * t, 8), :] = value

    stages = (
        (u, store(first, 3), 6, 6, 6, 6, lambda h, z, r, v: v),
        (first, store(second, 6), 3, 5, 5, 6, lambda h, z, r, v: 0.75 * u[h, at(z, r), :] + 0.25 * v),
        (
            second,
            put_out if initial else put_third,
            0,
            4,
            5,
            5,
            lambda h, z, r, v: (1.0 / 3.0) * u[h, at(z, r), :] + (2.0 / 3.0) * v,
        ),
    )
    for index, (src, dst, margin, tiles, face_tiles, triple_tiles, combine) in enumerate(stages):
        z_pass(src, side, acc, margin, tiles)
        y_pass(src, side, acc, scr, margin, tiles, face_tiles, triple_tiles, 2)
        x_pass(src, side, weight, acc, dst, x_scr, margin, tiles, combine)
        if index < 2:
            edge_rows((first, second)[index], DEEP - margin, 16 + 2 * margin, False, is_first, is_last)

    if initial:

        def slabs(k, carry):
            so_ref[k] = out_ref[k + 7 * odd_z]
            se_ref[k] = out_ref[k + 7 * (1 - odd_z)]
            return carry

        lax.fori_loop(0, DEEP, slabs, 0)
    else:
        lane = lax.broadcasted_iota(jnp.int32, (8, 128), 1)
        even = (lane & 1) == 0
        half = lane >> 1

        def merge(k, carry):
            for t in range(4):
                rows = pl.ds(k * 32 + 8 * t, 8)
                for h in range(2):
                    parts = [jnp.take_along_axis(third[p, rows, :], half + 64 * h, axis=1) for p in range(2)]
                    out_ref[k, 8 * t : 8 * t + 8, 128 * h : 128 * h + 128] = jnp.where(even, *parts)
            return carry

        lax.fori_loop(0, 16, merge, 0)


def split_kernel(own_ref, out_ref, so_ref, se_ref):
    odd_z = lax.rem(lax.axis_index("gz"), 2)
    lane = lax.broadcasted_iota(jnp.int32, (8, 128), 1)
    low = lane < 64
    twice = (lane & 63) * 2

    def plane(k, carry):
        for t in range(4):
            v = [own_ref[k, 8 * t : 8 * t + 8, 128 * h : 128 * h + 128] for h in range(2)]
            for p in range(2):
                parts = [jnp.take_along_axis(x, twice + p, axis=1) for x in v]
                out_ref[k, p, 8 * t : 8 * t + 8, :] = jnp.where(low, *parts)
        return carry

    lax.fori_loop(0, 16, plane, 0)

    def slabs(k, carry):
        so_ref[k] = out_ref[k + 7 * odd_z]
        se_ref[k] = out_ref[k + 7 * (1 - odd_z)]
        return carry

    lax.fori_loop(0, DEEP, slabs, 0)


def pack_kernel(own_ref, zo_ref, ze_ref, yo_ref, ye_ref):
    odd_z = lax.rem(lax.axis_index("gz"), 2)
    odd_y = lax.rem(lax.axis_index("gy"), 2)

    def fill(out, main, extra):
        def planes(ref, start, count):
            def one(k, carry):
                for h in range(2):
                    out[h, pl.ds(8 * (start + k), 8), :] = ref[k, h, main : main + 8, :]
                    out[h, pl.ds(272 + start + k, 1), :] = ref[k, h, extra : extra + 1, :]
                return carry

            lax.fori_loop(0, count, one, 0)

        planes(own_ref, DEEP, 16)
        planes(zo_ref, 25 * odd_z, DEEP)
        planes(ze_ref, 25 * (1 - odd_z), DEEP)
        out[:, 306:312, :] = jnp.zeros((2, 6, 128), f32)

    @pl.when(odd_y == 0)
    def _():
        fill(yo_ref, 0, 8)
        fill(ye_ref, 24, 23)

    @pl.when(odd_y == 1)
    def _():
        fill(yo_ref, 24, 23)
        fill(ye_ref, 0, 8)


def swaps(count, start, periodic):
    pairs = []
    for low in range(start, count, 2):
        if low + 1 < count or periodic:
            high = (low + 1) % count
            pairs += [(low, high), (high, low)]
    return pairs


VMEM = pl.BlockSpec(memory_space=pltpu.VMEM)
WORK = (2, 34 * PITCH, 128)


def per_device(level_set):
    n_z, n_y = lax.axis_size("gz"), lax.axis_size("gy")
    z_odd, z_even = swaps(n_z, 1, True), swaps(n_z, 0, True)
    y_odd, y_even = swaps(n_y, 1, False), swaps(n_y, 0, False)
    slab = jax.ShapeDtypeStruct((2, 312, 128), f32)
    deep = jax.ShapeDtypeStruct((DEEP, 2, 32, 128), f32)
    split = jax.ShapeDtypeStruct((16, 2, 32, 128), f32)
    params = pltpu.CompilerParams(vmem_limit_bytes=30 * 1024 * 1024)
    pack = pl.pallas_call(
        pack_kernel,
        out_shape=[slab, slab],
        in_specs=[VMEM] * 3,
        out_specs=[VMEM] * 2,
        compiler_params=params,
        name="pack_rows",
    )
    field, z_send_odd, z_send_even = pl.pallas_call(
        split_kernel,
        out_shape=[split, deep, deep],
        in_specs=[VMEM],
        out_specs=[VMEM] * 3,
        compiler_params=params,
        name="split_cells",
    )(level_set)
    keep = None
    for step in range(STEPS):
        zo = lax.ppermute(z_send_odd, "gz", z_odd)
        ze = lax.ppermute(z_send_even, "gz", z_even)
        y_send_odd, y_send_even = pack(field, zo, ze)
        yo = lax.ppermute(y_send_odd, "gy", y_odd)
        ye = lax.ppermute(y_send_even, "gy", y_even)
        initial = step == 0
        block = jax.ShapeDtypeStruct((16, 32, 256), f32)
        work = jax.ShapeDtypeStruct(WORK, f32)
        outs = [split, deep, deep, work] if initial else [block]
        args = (field, zo, ze, yo, ye) + (() if initial else (keep,))
        result = pl.pallas_call(
            functools.partial(step_kernel, initial),
            out_shape=outs,
            in_specs=[VMEM] * len(args),
            out_specs=[VMEM] * len(outs),
            scratch_shapes=[pltpu.VMEM(WORK, f32)] * 4
            + [pltpu.VMEM((2, 28 * 48, 128), f32)]
            + [pltpu.VMEM((4, 56, 128), f32)] * 6
            + [pltpu.VMEM((5, 48, 128), f32)] * 2
            + [pltpu.VMEM((2, 48, 128), f32)] * 2
            + [pltpu.VMEM((2, 512, 128), f32)],
            compiler_params=params,
            name="first_step" if initial else "next_step",
        )(*args)
        if initial:
            field, z_send_odd, z_send_even, keep = result
        else:
            (field,) = result
    return field


def solution(mesh):
    return jax.shard_map(
        per_device,
        mesh=mesh,
        in_specs=(P("gz", "gy", None),),
        out_specs=P("gz", "gy", None),
        check_vma=False,
    )
```

```python
import functools

import jax
import jax.numpy as jnp
from jax import lax
from jax.experimental import pallas as pl
from jax.experimental.pallas import tpu as pltpu
from jax.sharding import PartitionSpec as P

STEPS = 2
TAU = 0.3
EPS = 0.75e-6

DEEP = 9
PITCH = 64
ROW0 = 16
f32 = jnp.float32


def triple(g, h, curve):
    lean = 1.5 * curve
    mid = curve * curve + (0.75 * (g * h) + EPS)
    left = mid + lean * h
    right = mid - lean * g
    return left * left, mid * mid, right * right


def face(a, b, c, jump_low, jump_high, base_back, base_fore):
    p = b * c
    q = a * c
    r = a * b
    half = 0.5 * (p + r) + 3.0 * q
    pj = p * jump_low
    rj = r * jump_high
    back = base_back - (pj + 1.5 * rj) / (half + r)
    fore = base_fore - (1.5 * pj + rj) / (half + p)
    return back, fore


def upwind(back, fore, side):
    best = jnp.maximum(jnp.maximum(side * back, side * fore), 0.0)
    return best * best


def bases(center, low_slope, high_slope):
    six = 6.0 * center
    both = low_slope + high_slope
    return six + (both + high_slope), (both + low_slope) - six


def at(z, r, n=8):
    return pl.ds(z * PITCH + r, n)


def z_pass(src, side, acc, margin, r0, tiles, first_tile=0, tile_step=1):
    first = DEEP - margin
    last = DEEP + 16 + margin

    def column(i, carry):
        t = first_tile + tile_step * i
        r = r0 + 8 * t
        state = [dict(), dict()]
        for k in range(first - 1, last):
            for h in range(2):
                s = state[h]

                def u(z):
                    if ("u", z) not in s:
                        s["u", z] = src[h, at(z, r), :]
                    return s["u", z]

                def d(z):
                    if ("d", z) not in s:
                        s["d", z] = u(z + 1) - u(z)
                    return s["d", z]

                def e(z):
                    if ("e", z) not in s:
                        s["e", z] = d(z + 1) - d(z)
                    return s["e", z]

                def c(z):
                    if ("c", z) not in s:
                        s["c", z] = e(z) - e(z - 1)
                    return s["c", z]

                def j(z):
                    if ("j", z) not in s:
                        s["j", z] = c(z) - c(z - 1)
                    return s["j", z]

                def tr(z):
                    if ("t", z) not in s:
                        s["t", z] = triple(e(z - 1), e(z), c(z))
                    return s["t", z]

                base_back, base_fore = bases(d(k), e(k - 1), e(k))
                back, fore = face(
                    tr(k - 1)[0], tr(k)[1], tr(k + 1)[2], j(k), j(k + 1), base_back, base_fore
                )
                if k >= first:
                    acc[h, pl.ds((k - first) * 48 + 8 * t, 8), :] += upwind(
                        s["back"], fore, side[h, at(k, r), :]
                    )
                s["back"] = back
        return carry

    lax.fori_loop(0, tiles, column, 0)


def y_pass(src, side, rate_of, acc, scr, put, combine, margin, r0, tiles, face_tiles, triple_rows):
    first = DEEP - margin
    count = 16 + 2 * margin
    left_s, mid_s, right_s, curve_s, diff_s, fore_s = scr

    def two_planes(i, carry):
        for sub in range(2):
            zi = i * 2 + sub
            z = first + zi
            for h in range(2):
                slot = sub * 2 + h
                for row in triple_rows:
                    r = r0 - 2 + row
                    u0 = src[h, at(z, r - 1), :]
                    u1 = src[h, at(z, r), :]
                    u2 = src[h, at(z, r + 1), :]
                    u3 = src[h, at(z, r + 2), :]
                    d1 = u2 - u1
                    g = d1 - (u1 - u0)
                    e = (u3 - u2) - d1
                    curve = e - g
                    rows = pl.ds(row, 8)
                    left_s[slot, rows, :], mid_s[slot, rows, :], right_s[slot, rows, :] = triple(g, e, curve)
                    curve_s[slot, rows, :] = curve
                    diff_s[slot, rows, :] = d1
            for h in range(2):
                slot = sub * 2 + h
                backs = []
                for t in range(face_tiles):
                    lo, me, hi = pl.ds(8 * t, 8), pl.ds(8 * t + 1, 8), pl.ds(8 * t + 2, 8)
                    dl, dm, dh = diff_s[slot, lo, :], diff_s[slot, me, :], diff_s[slot, hi, :]
                    cm = curve_s[slot, me, :]
                    five = 5.0 * dm
                    back, fore = face(
                        left_s[slot, lo, :],
                        mid_s[slot, me, :],
                        right_s[slot, hi, :],
                        cm - curve_s[slot, lo, :],
                        curve_s[slot, hi, :] - cm,
                        five + ((dh + dh) - dl),
                        (dh - (dl + dl)) - five,
                    )
                    fore_s[slot, pl.ds(8 * t, 8), :] = fore
                    backs.append(back)
                for t in range(tiles):
                    r = r0 + 8 * t
                    fore = fore_s[slot, pl.ds(8 * t + 1, 8), :]
                    total = acc[h, pl.ds(zi * 48 + 8 * t, 8), :] + upwind(
                        backs[t], fore, side[h, at(z, r), :]
                    )
                    norm = total * lax.rsqrt(jnp.maximum(total, 1e-30))
                    stepped = src[h, at(z, r), :] + rate_of[h, at(z, r), :] * ((1.0 / 6.0) * norm - 1.0)
                    put(h, zi, t, r, combine(h, z, r, stepped))
        return carry

    lax.fori_loop(0, count // 2, two_planes, 0)


def x_pass(load, side, acc, scr, z0, count, acc0, r0, tile_list, unroll):
    lane = lax.broadcasted_iota(jnp.int32, (8, 128), 1)
    below_last = lane < 127
    below_two = lane < 126
    above_first = lane > 0
    shifted, finished = scr

    def shift(z, s):
        for t in tile_list:
            even, odd = load(0, z, r0 + 8 * t), load(1, z, r0 + 8 * t)
            rows = pl.ds(8 * t, 8)
            shifted[s, 0, rows, :] = jnp.where(above_first, pltpu.roll(even, 1, 1), even)
            shifted[s, 1, rows, :] = jnp.where(above_first, pltpu.roll(odd, 1, 1), even)
            shifted[s, 2, rows, :] = jnp.where(below_last, pltpu.roll(even, 127, 1), odd)
            odd_up = jnp.where(below_last, pltpu.roll(odd, 127, 1), odd)
            shifted[s, 3, rows, :] = odd_up
            shifted[s, 4, rows, :] = jnp.where(below_two, pltpu.roll(even, 126, 1), odd_up)

    def put(h, k, t, back, fore):
        wind = side[h, at(z0 + k, r0 + 8 * t), :]
        acc[h, pl.ds((acc0 + k) * 48 + 8 * t, 8), :] = upwind(back, fore, wind)

    def finish_even(k, s):
        for t in tile_list:
            rows = pl.ds(8 * t, 8)
            put(0, k, t, finished[s, 0, rows, :], finished[s, 1, rows, :])

    def faces(k, s):
        z = z0 + k
        for t in tile_list:
            rows = pl.ds(8 * t, 8)
            u = [
                shifted[s, 0, rows, :],
                shifted[s, 1, rows, :],
                load(0, z, r0 + 8 * t),
                load(1, z, r0 + 8 * t),
                shifted[s, 2, rows, :],
                shifted[s, 3, rows, :],
                shifted[s, 4, rows, :],
            ]
            d = [u[i + 1] - u[i] for i in range(6)]
            e = [d[i + 1] - d[i] for i in range(5)]
            c = [e[i + 1] - e[i] for i in range(4)]
            jump = [c[i + 1] - c[i] for i in range(3)]
            tri = [triple(e[i], e[i + 1], c[i]) for i in range(4)]
            back_even, fore_even = face(
                tri[0][0], tri[1][1], tri[2][2], jump[0], jump[1], *bases(d[2], e[1], e[2])
            )
            back_odd, fore_odd = face(
                tri[1][0], tri[2][1], tri[3][2], jump[1], jump[2], *bases(d[3], e[2], e[3])
            )
            p = tri[0][1] * tri[1][2]
            r = (1.5 * EPS * EPS) * tri[0][1]
            edge = (e[1] + e[1]) - (p * c[0] + r * jump[0]) / (
                (0.5 * p + r) + (3.0 * EPS * EPS) * tri[1][2]
            )
            finished[s, 0, rows, :] = jnp.where(above_first, pltpu.roll(back_odd, 1, 1), edge)
            finished[s, 1, rows, :] = fore_even
            put(1, k, t, back_even, fore_odd)

    shift(z0, 0)

    def planes(i, carry):
        for s in range(unroll):
            k = unroll * i + s
            shift(z0 + k + 1, (s + 1) % unroll)
            finish_even(jnp.maximum(k - 1, 0) if s == 0 else k - 1, (s - 1) % unroll)
            faces(k, s)
        return carry

    lax.fori_loop(0, count // unroll, planes, 0)
    finish_even(count - 1, unroll - 1)


def from_work(work):
    return lambda h, z, r: work[h, at(z, r), :]


def position():
    gz, gy = lax.axis_index("gz"), lax.axis_index("gy")
    return lax.rem(gz, 2), lax.rem(gy, 2), gy == 0, gy == lax.axis_size("gy") - 1


def load_planes(work, ref, start, count):
    def one(k, carry):
        for t in range(4):
            for h in range(2):
                work[h, at(start + k, ROW0 + 8 * t), :] = ref[k, h, 8 * t : 8 * t + 8, :]
        return carry

    lax.fori_loop(0, count, one, 0)


def load_rows(work, yo_ref, ye_ref, odd_y):
    def both(low, high):
        def one(z, carry):
            for h in range(2):
                work[h, at(z, ROW0 - 8), :] = low[h, pl.ds(8 * z, 8), :]
                work[h, at(z, ROW0 - 9, 1), :] = low[h, pl.ds(272 + z, 1), :]
                work[h, at(z, ROW0 + 32), :] = high[h, pl.ds(8 * z, 8), :]
                work[h, at(z, ROW0 + 40, 1), :] = high[h, pl.ds(272 + z, 1), :]
            return carry

        lax.fori_loop(0, 34, one, 0)

    @pl.when(odd_y == 0)
    def _():
        both(yo_ref, ye_ref)

    @pl.when(odd_y == 1)
    def _():
        both(ye_ref, yo_ref)


def signs(load, weight, side, z0, count, row_list):
    def one(k, carry):
        z = z0 + k
        for h in range(2):
            for r in row_list:
                v = load(h, z, r)
                weight[h, at(z, r), :] = (-TAU) * (v * lax.rsqrt(v * v + 1.0))
                side[h, at(z, r), :] = jnp.where(v >= 0.0, 1.0, -1.0)
        return carry

    lax.fori_loop(0, count, one, 0)


def edge_rows(work, start, count, far, is_first, is_last):
    @pl.when(is_first)
    def _():
        def one(k, carry):
            z = start + k
            for h in range(2):
                row = work[h, at(z, ROW0, 1), :]
                work[h, at(z, ROW0 - 8), :] = jnp.broadcast_to(row, (8, 128))
                if far:
                    work[h, at(z, ROW0 - 9, 1), :] = row
            return carry

        lax.fori_loop(0, count, one, 0)

    @pl.when(is_last)
    def _():
        def one(k, carry):
            z = start + k
            for h in range(2):
                row = work[h, at(z, ROW0 + 31, 1), :]
                work[h, at(z, ROW0 + 32), :] = jnp.broadcast_to(row, (8, 128))
                if far:
                    work[h, at(z, ROW0 + 40, 1), :] = row
            return carry

        lax.fori_loop(0, count, one, 0)


OWN_ROWS = tuple(ROW0 + 8 * t for t in range(4))
WIDE = ROW0 - 8
OWN_TILES = (1, 2, 3, 4)


def own_kernel(initial, own_ref, *refs):
    if initial:
        weight, side, acc, shifted, finished = refs

        def load(h, z, r):
            return own_ref[z - DEEP, h, pl.ds(r - ROW0, 8), :]

        signs(load, weight, side, DEEP, 16, OWN_ROWS)
    else:
        side, acc, shifted, finished = refs

    def load_clamped(h, z, r):
        return own_ref[jnp.minimum(z - DEEP, 15), h, pl.ds(r - ROW0, 8), :]

    x_pass(load_clamped, side, acc, (shifted, finished), DEEP, 16, 6, WIDE, OWN_TILES, 2)


def planes_kernel(initial, own_ref, zo_ref, ze_ref, *refs):
    if initial:
        _, _, _, weight, side, acc, u, shifted, finished = refs
    else:
        side, _, acc, u, shifted, finished = refs
    odd_z, _, _, _ = position()
    load_planes(u, own_ref, DEEP, 16)
    load_planes(u, zo_ref, 25 * odd_z, DEEP)
    load_planes(u, ze_ref, 25 * (1 - odd_z), DEEP)
    load = from_work(u)
    for z0 in (3, 25):
        if initial:
            signs(load, weight, side, z0, 6, OWN_ROWS)
        x_pass(load, side, acc, (shifted, finished), z0, 6, z0 - 3, WIDE, OWN_TILES, 2)
    z_pass(u, side, acc, 6, WIDE, 4, 1)


def rest_kernel(initial, yo_ref, ye_ref, *refs):
    refs = list(refs)
    if initial:
        out_ref, so_ref, se_ref, weight, side, acc, u = refs[4:11]
        refs = refs[11:]
    else:
        weight, side = refs[:2]
        out_ref, acc, u = refs[4:7]
        refs = refs[7:]
    first, second = refs[:2]
    scr = refs[2:8]
    x_scr = refs[8:10]
    third = refs[10]
    odd_z, odd_y, is_first, is_last = position()
    load_rows(u, yo_ref, ye_ref, odd_y)
    edge_rows(u, 0, 34, True, is_first, is_last)
    if initial:
        signs(from_work(u), weight, side, 3, 28, (WIDE, WIDE + 40))

    def store(work, start):
        def put(h, zi, t, r, value):
            work[h, at(start + zi, r), :] = value

        return put

    def put_out(h, zi, t, r, value):
        out_ref[zi, h, 8 * t : 8 * t + 8, :] = value

    def put_third(h, zi, t, r, value):
        third[h, pl.ds(zi * 32 + 8 * t, 8), :] = value

    def second_stage(h, z, r, v):
        return 0.75 * u[h, at(z, r), :] + 0.25 * v

    def third_stage(h, z, r, v):
        return (1.0 / 3.0) * u[h, at(z, r), :] + (2.0 / 3.0) * v

    x_pass(from_work(u), side, acc, x_scr, 3, 28, 0, WIDE, (0, 5), 4)
    z_pass(u, side, acc, 6, WIDE, 2, 0, 5)
    y_pass(
        u, side, weight, acc, scr, store(first, 3), lambda h, z, r, v: v, 6, WIDE, 6, 6, (1, 9, 17, 25, 33, 41)
    )
    edge_rows(first, 3, 28, False, is_first, is_last)
    x_pass(from_work(first), side, acc, x_scr, 6, 22, 0, ROW0 - 3, range(5), 2)
    z_pass(first, side, acc, 3, ROW0 - 3, 5)
    y_pass(
        first, side, weight, acc, scr, store(second, 6), second_stage, 3, ROW0 - 3, 5, 5, (0, 8, 16, 24, 32, 40)
    )
    edge_rows(second, 6, 22, False, is_first, is_last)
    x_pass(from_work(second), side, acc, x_scr, 9, 16, 0, ROW0, range(4), 2)
    z_pass(second, side, acc, 0, ROW0, 4)
    y_pass(
        second,
        side,
        weight,
        acc,
        scr,
        put_out if initial else put_third,
        third_stage,
        0,
        ROW0,
        4,
        5,
        (0, 8, 16, 24, 32),
    )

    if initial:

        def slabs(k, carry):
            so_ref[k] = out_ref[k + 7 * odd_z]
            se_ref[k] = out_ref[k + 7 * (1 - odd_z)]
            return carry

        lax.fori_loop(0, DEEP, slabs, 0)
    else:
        lane = lax.broadcasted_iota(jnp.int32, (8, 128), 1)
        even = (lane & 1) == 0
        half = lane >> 1

        def merge(k, carry):
            for t in range(4):
                rows = pl.ds(k * 32 + 8 * t, 8)
                for h in range(2):
                    parts = [jnp.take_along_axis(third[p, rows, :], half + 64 * h, axis=1) for p in range(2)]
                    out_ref[k, 8 * t : 8 * t + 8, 128 * h : 128 * h + 128] = jnp.where(even, *parts)
            return carry

        lax.fori_loop(0, 16, merge, 0)


def split_kernel(own_ref, out_ref, so_ref, se_ref):
    odd_z = lax.rem(lax.axis_index("gz"), 2)
    lane = lax.broadcasted_iota(jnp.int32, (8, 128), 1)
    low = lane < 64
    twice = (lane & 63) * 2

    def plane(k, carry):
        for t in range(4):
            v = [own_ref[k, 8 * t : 8 * t + 8, 128 * h : 128 * h + 128] for h in range(2)]
            for p in range(2):
                parts = [jnp.take_along_axis(x, twice + p, axis=1) for x in v]
                out_ref[k, p, 8 * t : 8 * t + 8, :] = jnp.where(low, *parts)
        return carry

    lax.fori_loop(0, 16, plane, 0)

    def slabs(k, carry):
        so_ref[k] = out_ref[k + 7 * odd_z]
        se_ref[k] = out_ref[k + 7 * (1 - odd_z)]
        return carry

    lax.fori_loop(0, DEEP, slabs, 0)


def pack_kernel(own_ref, zo_ref, ze_ref, yo_ref, ye_ref):
    odd_z = lax.rem(lax.axis_index("gz"), 2)
    odd_y = lax.rem(lax.axis_index("gy"), 2)

    def fill(out, main, extra):
        def planes(ref, start, count):
            def one(k, carry):
                for h in range(2):
                    out[h, pl.ds(8 * (start + k), 8), :] = ref[k, h, main : main + 8, :]
                    out[h, pl.ds(272 + start + k, 1), :] = ref[k, h, extra : extra + 1, :]
                return carry

            lax.fori_loop(0, count, one, 0)

        planes(own_ref, DEEP, 16)
        planes(zo_ref, 25 * odd_z, DEEP)
        planes(ze_ref, 25 * (1 - odd_z), DEEP)
        out[:, 306:312, :] = jnp.zeros((2, 6, 128), f32)

    @pl.when(odd_y == 0)
    def _():
        fill(yo_ref, 0, 8)
        fill(ye_ref, 24, 23)

    @pl.when(odd_y == 1)
    def _():
        fill(yo_ref, 24, 23)
        fill(ye_ref, 0, 8)


def swaps(count, start, periodic):
    pairs = []
    for low in range(start, count, 2):
        if low + 1 < count or periodic:
            high = (low + 1) % count
            pairs += [(low, high), (high, low)]
    return pairs


VMEM = pl.BlockSpec(memory_space=pltpu.VMEM)
WORK = (2, 34 * PITCH, 128)
ACC = (2, 28 * 48, 128)


def call(kernel, name, args, outs, scratch=(), aliases=None, cycles=1000):
    result = pl.pallas_call(
        kernel,
        out_shape=[jax.ShapeDtypeStruct(shape, f32) for shape in outs],
        in_specs=[VMEM] * len(args),
        out_specs=[VMEM] * len(outs),
        scratch_shapes=[pltpu.VMEM(shape, f32) for shape in scratch],
        input_output_aliases=aliases or {},
        compiler_params=pltpu.CompilerParams(vmem_limit_bytes=24 * 1024 * 1024),
        cost_estimate=pl.CostEstimate(flops=4096 * cycles, bytes_accessed=4096 * cycles, transcendentals=0),
        name=name,
    )(*args)
    return result


def per_device(level_set):
    n_z, n_y = lax.axis_size("gz"), lax.axis_size("gy")
    z_odd, z_even = swaps(n_z, 1, True), swaps(n_z, 0, True)
    y_odd, y_even = swaps(n_y, 1, False), swaps(n_y, 0, False)
    split, deep, slab = (16, 2, 32, 128), (DEEP, 2, 32, 128), (2, 312, 128)
    shifts = [(2, 5, 48, 128), (2, 2, 48, 128)]
    rest_scratch = [WORK] * 2 + [(4, 56, 128)] * 6 + [(4, 5, 48, 128), (4, 2, 48, 128), (2, 512, 128)]
    field, z_send_odd, z_send_even = call(split_kernel, "split_cells", (level_set,), [split, deep, deep])
    weight = side = None
    for step in range(STEPS):
        initial = step == 0
        zo = lax.ppermute(z_send_odd, "gz", z_odd)
        ze = lax.ppermute(z_send_even, "gz", z_even)
        own = functools.partial(own_kernel, initial)
        planes = functools.partial(planes_kernel, initial)
        rest = functools.partial(rest_kernel, initial)
        if initial:
            weight, side, acc = call(own, "own_planes", (field,), [WORK, WORK, ACC], shifts, cycles=4000)
        else:
            (acc,) = call(own, "own_planes_next", (field, side), [ACC], shifts, cycles=4000)
        y_send_odd, y_send_even = call(pack_kernel, "pack_rows", (field, zo, ze), [slab, slab])
        yo = lax.ppermute(y_send_odd, "gy", y_odd)
        ye = lax.ppermute(y_send_even, "gy", y_even)
        if initial:
            weight, side, acc, u = call(
                planes,
                "ghost_planes",
                (field, zo, ze, weight, side, acc),
                [WORK, WORK, ACC, WORK],
                shifts,
                {3: 0, 4: 1, 5: 2},
                8000,
            )
            field, z_send_odd, z_send_even, weight, side, _, _ = call(
                rest,
                "first_step",
                (yo, ye, weight, side, acc, u),
                [split, deep, deep, WORK, WORK, ACC, WORK],
                rest_scratch,
                {2: 3, 3: 4, 4: 5, 5: 6},
                30000,
            )
        else:
            acc, u = call(
                planes,
                "ghost_planes_next",
                (field, zo, ze, side, acc),
                [ACC, WORK],
                shifts,
                {4: 0},
                8000,
            )
            field, _, _ = call(
                rest,
                "next_step",
                (yo, ye, weight, side, acc, u),
                [(16, 32, 256), ACC, WORK],
                rest_scratch,
                {4: 1, 5: 2},
                30000,
            )
    return field


def solution(mesh):
    return jax.shard_map(
        per_device,
        mesh=mesh,
        in_specs=(P("gz", "gy", None),),
        out_specs=P("gz", "gy", None),
        check_vma=False,
    )
```

```python
import functools

import jax
import jax.numpy as jnp
from jax import lax
from jax.experimental import pallas as pl
from jax.experimental.pallas import tpu as pltpu
from jax.sharding import PartitionSpec as P

STEPS = 2
TAU = 0.3
EPS = 0.75e-6

DEEP = 9
PITCH = 64
ROW0 = 16
f32 = jnp.float32


def triple(g, h, curve):
    lean = 1.5 * curve
    mid = curve * curve + (0.75 * (g * h) + EPS)
    left = mid + lean * h
    right = mid - lean * g
    return left * left, mid * mid, right * right


def face(a, b, c, jump_low, jump_high, base_back, base_fore):
    p = b * c
    q = a * c
    r = a * b
    half = 0.5 * (p + r) + 3.0 * q
    pj = p * jump_low
    rj = r * jump_high
    back = base_back - (pj + 1.5 * rj) / (half + r)
    fore = base_fore - (1.5 * pj + rj) / (half + p)
    return back, fore


def upwind(back, fore, side):
    best = jnp.maximum(jnp.maximum(side * back, side * fore), 0.0)
    return best * best


def bases(center, low_slope, high_slope):
    six = 6.0 * center
    both = low_slope + high_slope
    return six + (both + high_slope), (both + low_slope) - six


def at(z, r, n=8):
    return pl.ds(z * PITCH + r, n)


def z_pass(src, side, acc, margin, r0, tiles, first_tile=0, tile_step=1, acc0=0, fresh=False):
    first = DEEP - margin
    last = DEEP + 16 + margin

    def column(i, carry):
        t = first_tile + tile_step * i
        r = r0 + 8 * t
        state = [dict(), dict()]
        for k in range(first - 1, last):
            for h in range(2):
                s = state[h]

                def u(z):
                    if ("u", z) not in s:
                        s["u", z] = src[h, at(z, r), :]
                    return s["u", z]

                def d(z):
                    if ("d", z) not in s:
                        s["d", z] = u(z + 1) - u(z)
                    return s["d", z]

                def e(z):
                    if ("e", z) not in s:
                        s["e", z] = d(z + 1) - d(z)
                    return s["e", z]

                def c(z):
                    if ("c", z) not in s:
                        s["c", z] = e(z) - e(z - 1)
                    return s["c", z]

                def j(z):
                    if ("j", z) not in s:
                        s["j", z] = c(z) - c(z - 1)
                    return s["j", z]

                def tr(z):
                    if ("t", z) not in s:
                        s["t", z] = triple(e(z - 1), e(z), c(z))
                    return s["t", z]

                base_back, base_fore = bases(d(k), e(k - 1), e(k))
                back, fore = face(
                    tr(k - 1)[0], tr(k)[1], tr(k + 1)[2], j(k), j(k + 1), base_back, base_fore
                )
                if k >= first:
                    rows = pl.ds((acc0 + k - first) * 48 + 8 * t, 8)
                    share = upwind(s["back"], fore, side[h, at(k, r), :])
                    acc[h, rows, :] = share if fresh else acc[h, rows, :] + share
                s["back"] = back
        return carry

    lax.fori_loop(0, tiles, column, 0)


def y_plane(src, side, rate_of, acc, scr, put, combine, margin, r0, tiles, face_tiles, rows):
    first = DEEP - margin
    left_s, mid_s, right_s, curve_s, diff_s, slope_s, fore_s = scr
    triple_rows, slope_rows, diff_rows = rows

    def plane(zi, sub):
        z = first + zi
        for h in range(2):
            slot = sub * 2 + h
            for row in diff_rows:
                r = r0 - 2 + row
                diff_s[slot, pl.ds(row + 1, 8), :] = src[h, at(z, r + 1), :] - src[h, at(z, r), :]
            for row in slope_rows:
                above, below = diff_s[slot, pl.ds(row + 2, 8), :], diff_s[slot, pl.ds(row + 1, 8), :]
                slope_s[slot, pl.ds(row + 1, 8), :] = above - below
            for row in triple_rows:
                g, e = slope_s[slot, pl.ds(row, 8), :], slope_s[slot, pl.ds(row + 1, 8), :]
                curve = e - g
                rows = pl.ds(row, 8)
                left_s[slot, rows, :], mid_s[slot, rows, :], right_s[slot, rows, :] = triple(g, e, curve)
                curve_s[slot, rows, :] = curve
        for h in range(2):
            slot = sub * 2 + h
            backs = []
            for t in range(face_tiles):
                lo, me, hi = pl.ds(8 * t, 8), pl.ds(8 * t + 1, 8), pl.ds(8 * t + 2, 8)
                cm = curve_s[slot, me, :]
                back, fore = face(
                    left_s[slot, lo, :],
                    mid_s[slot, me, :],
                    right_s[slot, hi, :],
                    cm - curve_s[slot, lo, :],
                    curve_s[slot, hi, :] - cm,
                    *bases(diff_s[slot, hi, :], slope_s[slot, me, :], slope_s[slot, hi, :]),
                )
                fore_s[slot, pl.ds(8 * t, 8), :] = fore
                backs.append(back)
            for t in range(tiles):
                r = r0 + 8 * t
                fore = fore_s[slot, pl.ds(8 * t + 1, 8), :]
                total = acc[h, pl.ds(zi * 48 + 8 * t, 8), :] + upwind(
                    backs[t], fore, side[h, at(z, r), :]
                )
                norm = total * lax.rsqrt(jnp.maximum(total, 1e-30))
                stepped = src[h, at(z, r), :] + rate_of[h, at(z, r), :] * ((1.0 / 6.0) * norm - 1.0)
                put(h, zi, t, r, combine(h, z, r, stepped))

    return plane


def y_pass(count, plane):
    def two_planes(i, carry):
        plane(2 * i, 0)
        plane(2 * i + 1, 1)
        return carry

    lax.fori_loop(0, count // 2, two_planes, 0)


def x_parts(load, side, acc, scr, z0, acc0, r0, tile_list, fresh):
    lane = lax.broadcasted_iota(jnp.int32, (8, 128), 1)
    below_last = lane < 127
    below_two = lane < 126
    above_first = lane > 0
    shifted, finished = scr

    def shift(z, s):
        for t in tile_list:
            even, odd = load(0, z, r0 + 8 * t), load(1, z, r0 + 8 * t)
            rows = pl.ds(8 * t, 8)
            shifted[s, 0, rows, :] = jnp.where(above_first, pltpu.roll(even, 1, 1), even)
            shifted[s, 1, rows, :] = jnp.where(above_first, pltpu.roll(odd, 1, 1), even)
            shifted[s, 2, rows, :] = jnp.where(below_last, pltpu.roll(even, 127, 1), odd)
            odd_up = jnp.where(below_last, pltpu.roll(odd, 127, 1), odd)
            shifted[s, 3, rows, :] = odd_up
            shifted[s, 4, rows, :] = jnp.where(below_two, pltpu.roll(even, 126, 1), odd_up)

    def put(h, k, t, back, fore):
        wind = side[h, at(z0 + k, r0 + 8 * t), :]
        rows = pl.ds((acc0 + k) * 48 + 8 * t, 8)
        share = upwind(back, fore, wind)
        acc[h, rows, :] = share if fresh else acc[h, rows, :] + share

    def finish_even(k, s):
        for t in tile_list:
            rows = pl.ds(8 * t, 8)
            put(0, k, t, finished[s, 0, rows, :], finished[s, 1, rows, :])

    def faces(k, s):
        z = z0 + k
        for t in tile_list:
            rows = pl.ds(8 * t, 8)
            u = [
                shifted[s, 0, rows, :],
                shifted[s, 1, rows, :],
                load(0, z, r0 + 8 * t),
                load(1, z, r0 + 8 * t),
                shifted[s, 2, rows, :],
                shifted[s, 3, rows, :],
                shifted[s, 4, rows, :],
            ]
            d = [u[i + 1] - u[i] for i in range(6)]
            e = [d[i + 1] - d[i] for i in range(5)]
            c = [e[i + 1] - e[i] for i in range(4)]
            jump = [c[i + 1] - c[i] for i in range(3)]
            tri = [triple(e[i], e[i + 1], c[i]) for i in range(4)]
            back_even, fore_even = face(
                tri[0][0], tri[1][1], tri[2][2], jump[0], jump[1], *bases(d[2], e[1], e[2])
            )
            back_odd, fore_odd = face(
                tri[1][0], tri[2][1], tri[3][2], jump[1], jump[2], *bases(d[3], e[2], e[3])
            )
            p = tri[0][1] * tri[1][2]
            r = (1.5 * EPS * EPS) * tri[0][1]
            edge = (e[1] + e[1]) - (p * c[0] + r * jump[0]) / (
                (0.5 * p + r) + (3.0 * EPS * EPS) * tri[1][2]
            )
            finished[s, 0, rows, :] = jnp.where(above_first, pltpu.roll(back_odd, 1, 1), edge)
            finished[s, 1, rows, :] = fore_even
            put(1, k, t, back_even, fore_odd)

    return lambda k, s: shift(z0 + k, s), finish_even, faces


def x_pass(load, side, acc, scr, z0, count, acc0, r0, tile_list):
    shift, finish_even, faces = x_parts(load, side, acc, scr, z0, acc0, r0, tile_list, True)
    shift(0, 0)

    def planes(i, carry):
        for s in range(2):
            k = 2 * i + s
            shift(k + 1, (s + 1) % 2)
            finish_even(jnp.maximum(k - 1, 0) if s == 0 else k - 1, (s - 1) % 2)
            faces(k, s)
        return carry

    lax.fori_loop(0, count // 2, planes, 0)
    finish_even(count - 1, 1)


def xy_pass(load, side, acc, scr, z0, count, r0, tile_list, plane):
    shift, finish_even, faces = x_parts(load, side, acc, scr, z0, 0, r0, tile_list, False)
    shift(0, 0)
    shift(1, 1)
    faces(0, 0)
    shift(2, 0)
    finish_even(0, 0)
    faces(1, 1)

    def planes(i, carry):
        for s in range(2):
            k = 2 * i + s
            shift(k + 1, (s + 1) % 2)
            finish_even(k - 1, (s - 1) % 2)
            faces(k, s)
            plane(k - 2, s)
        return carry

    lax.fori_loop(1, count // 2, planes, 0)
    finish_even(count - 1, 1)
    plane(count - 2, 0)
    plane(count - 1, 1)


def from_work(work):
    return lambda h, z, r: work[h, at(z, r), :]


def position():
    gz, gy = lax.axis_index("gz"), lax.axis_index("gy")
    return lax.rem(gz, 2), lax.rem(gy, 2), gy == 0, gy == lax.axis_size("gy") - 1


def load_planes(work, ref, start, count):
    def one(k, carry):
        for t in range(4):
            for h in range(2):
                work[h, at(start + k, ROW0 + 8 * t), :] = ref[k, h, 8 * t : 8 * t + 8, :]
        return carry

    lax.fori_loop(0, count, one, 0)


NINTH, NEXT, FAR, SLAB = 128, 144, 192, 216


def slab_planes():
    near = [(DEEP - 3 + i if i < 3 else DEEP + 13 + i, NEXT + 8 * i, 8) for i in range(6)]
    far = [(DEEP - 6 + i if i < 3 else DEEP + 16 + i, FAR + 4 * i, 4) for i in range(6)]
    return near + far


def load_rows(work, yo_ref, ye_ref, odd_y):
    def both(low, high):
        def own(i, carry):
            for sub in range(2):
                k = 2 * i + sub
                z = DEEP + k
                for h in range(2):
                    work[h, at(z, ROW0 - 8), :] = low[h, pl.ds(8 * k, 8), :]
                    work[h, at(z, ROW0 - 9, 1), :] = low[h, pl.ds(NINTH + k, 1), :]
                    work[h, at(z, ROW0 + 32), :] = high[h, pl.ds(8 * k, 8), :]
                    work[h, at(z, ROW0 + 40, 1), :] = high[h, pl.ds(NINTH + k, 1), :]
            return carry

        lax.fori_loop(0, 8, own, 0)
        for z, row, n in slab_planes():
            for h in range(2):
                work[h, at(z, ROW0 - n, n), :] = low[h, row : row + n, :]
                work[h, at(z, ROW0 + 32, n), :] = high[h, row : row + n, :]

    @pl.when(odd_y == 0)
    def _():
        both(yo_ref, ye_ref)

    @pl.when(odd_y == 1)
    def _():
        both(ye_ref, yo_ref)


def signs(load, weight, side, z0, count, row_list):
    def one(k, carry):
        z = z0 + k
        for h in range(2):
            for r in row_list:
                v = load(h, z, r)
                weight[h, at(z, r), :] = (-TAU) * (v * lax.rsqrt(v * v + 1.0))
                side[h, at(z, r), :] = jnp.where(v >= 0.0, 1.0, -1.0)
        return carry

    lax.fori_loop(0, count, one, 0)


def edge_rows(work, start, count, far, is_first, is_last):
    @pl.when(is_first)
    def _():
        def one(k, carry):
            z = start + k
            for h in range(2):
                row = work[h, at(z, ROW0, 1), :]
                work[h, at(z, ROW0 - 8), :] = jnp.broadcast_to(row, (8, 128))
                if far:
                    work[h, at(z, ROW0 - 9, 1), :] = row
            return carry

        lax.fori_loop(0, count, one, 0)

    @pl.when(is_last)
    def _():
        def one(k, carry):
            z = start + k
            for h in range(2):
                row = work[h, at(z, ROW0 + 31, 1), :]
                work[h, at(z, ROW0 + 32), :] = jnp.broadcast_to(row, (8, 128))
                if far:
                    work[h, at(z, ROW0 + 40, 1), :] = row
            return carry

        lax.fori_loop(0, count, one, 0)


OWN_ROWS = tuple(ROW0 + 8 * t for t in range(4))
WIDE = ROW0 - 8
OWN_TILES = (1, 2, 3, 4)


def own_kernel(initial, own_ref, *refs):
    if initial:
        weight, side, acc, shifted, finished = refs

        def load(h, z, r):
            return own_ref[z - DEEP, h, pl.ds(r - ROW0, 8), :]

        signs(load, weight, side, DEEP, 16, OWN_ROWS)
    else:
        side, acc, shifted, finished = refs

    def load_clamped(h, z, r):
        return own_ref[jnp.minimum(z - DEEP, 15), h, pl.ds(r - ROW0, 8), :]

    x_pass(load_clamped, side, acc, (shifted, finished), DEEP, 16, 6, WIDE, OWN_TILES)


def planes_kernel(initial, own_ref, zo_ref, ze_ref, *refs):
    if initial:
        _, _, _, weight, side, acc, u, shifted, finished = refs
    else:
        side, _, acc, u, shifted, finished = refs
    odd_z, _, _, _ = position()
    load_planes(u, own_ref, DEEP, 16)
    load_planes(u, zo_ref, 25 * odd_z, DEEP)
    load_planes(u, ze_ref, 25 * (1 - odd_z), DEEP)
    load = from_work(u)
    for z0 in (3, 25):
        if initial:
            signs(load, weight, side, z0, 6, OWN_ROWS)
        x_pass(load, side, acc, (shifted, finished), z0, 6, z0 - 3, WIDE, OWN_TILES)
    z_pass(u, side, acc, 6, WIDE, 4, 1)


def rest_kernel(initial, yo_ref, ye_ref, *refs):
    refs = list(refs)
    if initial:
        out_ref, so_ref, se_ref, weight, side, acc, u = refs[4:11]
        refs = refs[11:]
    else:
        weight, side = refs[:2]
        out_ref, acc, u = refs[4:7]
        refs = refs[7:]
    first, second = refs[:2]
    scr = refs[2:9]
    x_scr = refs[9:11]
    third = refs[11]
    if not initial:
        merged, sems = refs[12:14]
    odd_z, odd_y, is_first, is_last = position()
    load_rows(u, yo_ref, ye_ref, odd_y)
    edge_rows(u, 0, 34, True, is_first, is_last)
    if initial:
        signs(from_work(u), weight, side, 6, 22, (WIDE, WIDE + 40))

    def store(work, start):
        def put(h, zi, t, r, value):
            work[h, at(start + zi, r), :] = value

        return put

    def put_out(h, zi, t, r, value):
        out_ref[zi, h, 8 * t : 8 * t + 8, :] = value

    def put_third(h, zi, t, r, value):
        third[h, pl.ds(zi * 32 + 8 * t, 8), :] = value

    def second_stage(h, z, r, v):
        return 0.75 * u[h, at(z, r), :] + 0.25 * v

    def third_stage(h, z, r, v):
        return (1.0 / 3.0) * u[h, at(z, r), :] + (2.0 / 3.0) * v

    z_pass(u, side, acc, 3, WIDE, 2, 0, 5, 3, True)
    rows = (1, 9, 17, 25, 33, 41)
    rows = rows, rows, rows + (42,)
    plane = y_plane(u, side, weight, acc, scr, store(first, 3), lambda h, z, r, v: v, 6, WIDE, 6, 6, rows)
    xy_pass(from_work(u), side, acc, x_scr, 3, 28, WIDE, (0, 5), plane)
    edge_rows(first, 3, 28, False, is_first, is_last)
    z_pass(first, side, acc, 3, ROW0 - 3, 5, fresh=True)
    rows = tuple(range(0, 48, 8))
    below = tuple(range(-1, 47, 8))
    plane = y_plane(
        first, side, weight, acc, scr, store(second, 6), second_stage, 3, ROW0 - 3, 5, 5, (rows, below, below)
    )
    xy_pass(from_work(first), side, acc, x_scr, 6, 22, ROW0 - 3, range(5), plane)
    edge_rows(second, 6, 22, False, is_first, is_last)
    z_pass(second, side, acc, 0, ROW0, 4, fresh=True)
    put = put_out if initial else put_third
    rows, below = rows[:5], below[:5]
    plane = y_plane(second, side, weight, acc, scr, put, third_stage, 0, ROW0, 4, 5, (rows, below, below))
    xy_pass(from_work(second), side, acc, x_scr, 9, 16, ROW0, range(4), plane)

    if initial:

        def slabs(k, carry):
            so_ref[k] = out_ref[k + 7 * odd_z]
            se_ref[k] = out_ref[k + 7 * (1 - odd_z)]
            return carry

        lax.fori_loop(0, DEEP, slabs, 0)
    else:
        lane = lax.broadcasted_iota(jnp.int32, (8, 128), 1)
        even = (lane & 1) == 0
        half = lane >> 1
        copies = []
        for chunk in range(4):
            for k in range(4 * chunk, 4 * chunk + 4):
                for t in range(4):
                    rows = pl.ds(k * 32 + 8 * t, 8)
                    for h in range(2):
                        parts = [
                            jnp.take_along_axis(third[p, rows, :], half + 64 * h, axis=1) for p in range(2)
                        ]
                        merged[k, 8 * t : 8 * t + 8, 128 * h : 128 * h + 128] = jnp.where(even, *parts)
            planes = pl.ds(4 * chunk, 4)
            copies.append(pltpu.make_async_copy(merged.at[planes], out_ref.at[planes], sems.at[chunk]))
            copies[-1].start()
        for copy in copies:
            copy.wait()


def split_kernel(own_ref, out_ref, so_ref, se_ref):
    odd_z = lax.rem(lax.axis_index("gz"), 2)
    lane = lax.broadcasted_iota(jnp.int32, (8, 128), 1)
    low = lane < 64
    twice = (lane & 63) * 2
    for chunk in range(4):
        for k in range(4 * chunk, 4 * chunk + 4):
            for t in range(4):
                v = [own_ref[k, 8 * t : 8 * t + 8, 128 * h : 128 * h + 128] for h in range(2)]
                for p in range(2):
                    parts = [jnp.take_along_axis(x, twice + p, axis=1) for x in v]
                    out_ref[k, p, 8 * t : 8 * t + 8, :] = jnp.where(low, *parts)

    def slabs(k, carry):
        so_ref[k] = out_ref[k + 7 * odd_z]
        se_ref[k] = out_ref[k + 7 * (1 - odd_z)]
        return carry

    lax.fori_loop(0, DEEP, slabs, 0)


def pack_kernel(own_ref, zo_ref, ze_ref, yo_ref, ye_ref):
    odd_z, odd_y, _, _ = position()

    def fill(out, top, low_ref, high_ref):
        main, ninth, short = (24, 23, 28) if top else (0, 8, 0)

        def own(i, carry):
            for sub in range(2):
                k = 2 * i + sub
                for h in range(2):
                    out[h, pl.ds(8 * k, 8), :] = own_ref[k, h, main : main + 8, :]
                    out[h, pl.ds(NINTH + k, 1), :] = own_ref[k, h, ninth : ninth + 1, :]
            return carry

        lax.fori_loop(0, 8, own, 0)
        for z, row, n in slab_planes():
            ref, k = (low_ref, z) if z < DEEP else (high_ref, z - DEEP - 16)
            first = main if n == 8 else short
            for h in range(2):
                out[h, row : row + n, :] = ref[k, h, first : first + n, :]

    for z_parity in range(2):
        for y_parity in range(2):

            @pl.when((odd_z == z_parity) & (odd_y == y_parity))
            def _(z_parity=z_parity, y_parity=y_parity):
                low_ref, high_ref = (ze_ref, zo_ref) if z_parity else (zo_ref, ze_ref)
                fill(yo_ref, y_parity == 1, low_ref, high_ref)
                fill(ye_ref, y_parity == 0, low_ref, high_ref)


def swaps(count, start, periodic):
    pairs = []
    for low in range(start, count, 2):
        if low + 1 < count or periodic:
            high = (low + 1) % count
            pairs += [(low, high), (high, low)]
    return pairs


VMEM = pl.BlockSpec(memory_space=pltpu.VMEM)
WORK = (2, 34 * PITCH, 128)
ACC = (2, 28 * 48, 128)


def call(kernel, name, args, outs, scratch=(), aliases=None, cycles=1000, hbm=()):
    anywhere = pl.BlockSpec(memory_space=pltpu.HBM)
    more = [pltpu.VMEM((16, 32, 256), f32), pltpu.SemaphoreType.DMA((4,))] if hbm else []
    return pl.pallas_call(
        kernel,
        out_shape=[jax.ShapeDtypeStruct(shape, f32) for shape in outs],
        in_specs=[anywhere if ("in", i) == hbm else VMEM for i in range(len(args))],
        out_specs=[anywhere if ("out", i) == hbm else VMEM for i in range(len(outs))],
        scratch_shapes=[pltpu.VMEM(shape, f32) for shape in scratch] + more,
        input_output_aliases=aliases or {},
        compiler_params=pltpu.CompilerParams(vmem_limit_bytes=24 * 1024 * 1024),
        cost_estimate=pl.CostEstimate(flops=4096 * cycles, bytes_accessed=4096 * cycles, transcendentals=0),
        name=name,
    )(*args)


def per_device(level_set):
    n_z, n_y = lax.axis_size("gz"), lax.axis_size("gy")
    z_odd, z_even = swaps(n_z, 1, True), swaps(n_z, 0, True)
    y_odd, y_even = swaps(n_y, 1, False), swaps(n_y, 0, False)
    split, deep, slab = (16, 2, 32, 128), (DEEP, 2, 32, 128), (2, SLAB, 128)
    shifts = [(2, 5, 48, 128), (2, 2, 48, 128)]
    rest_scratch = [WORK] * 2 + [(4, 56, 128)] * 7 + shifts + [(2, 512, 128)]
    field, z_send_odd, z_send_even = call(split_kernel, "split_cells", (level_set,), [split, deep, deep])
    weight = side = None
    for step in range(STEPS):
        initial = step == 0
        zo = lax.ppermute(z_send_odd, "gz", z_odd)
        ze = lax.ppermute(z_send_even, "gz", z_even)
        own = functools.partial(own_kernel, initial)
        planes = functools.partial(planes_kernel, initial)
        rest = functools.partial(rest_kernel, initial)
        if initial:
            weight, side, acc = call(own, "own_planes", (field,), [WORK, WORK, ACC], shifts, cycles=4000)
        else:
            (acc,) = call(own, "own_planes_next", (field, side), [ACC], shifts, cycles=4000)
        y_send_odd, y_send_even = call(pack_kernel, "pack_rows", (field, zo, ze), [slab, slab])
        yo = lax.ppermute(y_send_odd, "gy", y_odd)
        ye = lax.ppermute(y_send_even, "gy", y_even)
        if initial:
            weight, side, acc, u = call(
                planes,
                "ghost_planes",
                (field, zo, ze, weight, side, acc),
                [WORK, WORK, ACC, WORK],
                shifts,
                {3: 0, 4: 1, 5: 2},
                8000,
            )
            field, z_send_odd, z_send_even, weight, side, _, _ = call(
                rest,
                "first_step",
                (yo, ye, weight, side, acc, u),
                [split, deep, deep, WORK, WORK, ACC, WORK],
                rest_scratch,
                {2: 3, 3: 4, 4: 5, 5: 6},
                30000,
            )
        else:
            acc, u = call(
                planes,
                "ghost_planes_next",
                (field, zo, ze, side, acc),
                [ACC, WORK],
                shifts,
                {4: 0},
                8000,
            )
            field, _, _ = call(
                rest,
                "next_step",
                (yo, ye, weight, side, acc, u),
                [(16, 32, 256), ACC, WORK],
                rest_scratch,
                {4: 1, 5: 2},
                30000,
                ("out", 0),
            )
    return field


def solution(mesh):
    return jax.shard_map(
        per_device,
        mesh=mesh,
        in_specs=(P("gz", "gy", None),),
        out_specs=P("gz", "gy", None),
        check_vma=False,
    )
```

```python
import functools

import jax
import jax.numpy as jnp
from jax import lax
from jax.experimental import pallas as pl
from jax.experimental.pallas import tpu as pltpu
from jax.sharding import PartitionSpec as P

STEPS = 2
TAU = 0.3
EPS = 0.75e-6

DEEP = 9
PITCH = 64
ROW0 = 16
f32 = jnp.float32


def triple(g, h, curve):
    lean = 1.5 * curve
    mid = curve * curve + (0.75 * (g * h) + EPS)
    left = mid + lean * h
    right = mid - lean * g
    return left * left, mid * mid, right * right


def face(a, b, c, jump_low, jump_high, base_back, base_fore):
    p = b * c
    q = a * c
    r = a * b
    half = 0.5 * (p + r) + 3.0 * q
    pj = p * jump_low
    rj = r * jump_high
    back = base_back - (pj + 1.5 * rj) / (half + r)
    fore = base_fore - (1.5 * pj + rj) / (half + p)
    return back, fore


def upwind(back, fore, side):
    best = jnp.maximum(jnp.maximum(side * back, side * fore), 0.0)
    return best * best


def bases(center, low_slope, high_slope):
    six = 6.0 * center
    both = low_slope + high_slope
    return six + (both + high_slope), (both + low_slope) - six


def at(z, r, n=8):
    return pl.ds(z * PITCH + r, n)


def z_pass(src, side, acc, margin, r0, tiles, first_tile=0, tile_step=1, acc0=0, fresh=False):
    first = DEEP - margin
    last = DEEP + 16 + margin

    def column(i, carry):
        t = first_tile + tile_step * i
        r = r0 + 8 * t
        state = [dict(), dict()]
        for k in range(first - 1, last):
            for h in range(2):
                s = state[h]

                def u(z):
                    if ("u", z) not in s:
                        s["u", z] = src[h, at(z, r), :]
                    return s["u", z]

                def d(z):
                    if ("d", z) not in s:
                        s["d", z] = u(z + 1) - u(z)
                    return s["d", z]

                def e(z):
                    if ("e", z) not in s:
                        s["e", z] = d(z + 1) - d(z)
                    return s["e", z]

                def c(z):
                    if ("c", z) not in s:
                        s["c", z] = e(z) - e(z - 1)
                    return s["c", z]

                def j(z):
                    if ("j", z) not in s:
                        s["j", z] = c(z) - c(z - 1)
                    return s["j", z]

                def tr(z):
                    if ("t", z) not in s:
                        s["t", z] = triple(e(z - 1), e(z), c(z))
                    return s["t", z]

                base_back, base_fore = bases(d(k), e(k - 1), e(k))
                back, fore = face(
                    tr(k - 1)[0], tr(k)[1], tr(k + 1)[2], j(k), j(k + 1), base_back, base_fore
                )
                if k >= first:
                    rows = pl.ds((acc0 + k - first) * 48 + 8 * t, 8)
                    share = upwind(s["back"], fore, side[h, at(k, r), :])
                    acc[h, rows, :] = share if fresh else acc[h, rows, :] + share
                s["back"] = back
        return carry

    lax.fori_loop(0, tiles, column, 0)


def y_plane(src, side, rate_of, acc, scr, put, combine, margin, r0, tiles, face_tiles, rows):
    first = DEEP - margin
    left_s, mid_s, right_s, curve_s, diff_s, slope_s, fore_s = scr
    triple_rows, slope_rows, diff_rows = rows

    def plane(zi, sub):
        z = first + zi
        for h in range(2):
            slot = sub * 2 + h
            for row in diff_rows:
                r = r0 - 2 + row
                diff_s[slot, pl.ds(row + 1, 8), :] = src[h, at(z, r + 1), :] - src[h, at(z, r), :]
            for row in slope_rows:
                above, below = diff_s[slot, pl.ds(row + 2, 8), :], diff_s[slot, pl.ds(row + 1, 8), :]
                slope_s[slot, pl.ds(row + 1, 8), :] = above - below
            for row in triple_rows:
                g, e = slope_s[slot, pl.ds(row, 8), :], slope_s[slot, pl.ds(row + 1, 8), :]
                curve = e - g
                rows = pl.ds(row, 8)
                left_s[slot, rows, :], mid_s[slot, rows, :], right_s[slot, rows, :] = triple(g, e, curve)
                curve_s[slot, rows, :] = curve
        for h in range(2):
            slot = sub * 2 + h
            backs = []
            for t in range(face_tiles):
                lo, me, hi = pl.ds(8 * t, 8), pl.ds(8 * t + 1, 8), pl.ds(8 * t + 2, 8)
                cm = curve_s[slot, me, :]
                back, fore = face(
                    left_s[slot, lo, :],
                    mid_s[slot, me, :],
                    right_s[slot, hi, :],
                    cm - curve_s[slot, lo, :],
                    curve_s[slot, hi, :] - cm,
                    *bases(diff_s[slot, hi, :], slope_s[slot, me, :], slope_s[slot, hi, :]),
                )
                fore_s[slot, pl.ds(8 * t, 8), :] = fore
                backs.append(back)
            for t in range(tiles):
                r = r0 + 8 * t
                fore = fore_s[slot, pl.ds(8 * t + 1, 8), :]
                total = acc[h, pl.ds(zi * 48 + 8 * t, 8), :] + upwind(
                    backs[t], fore, side[h, at(z, r), :]
                )
                norm = total * lax.rsqrt(jnp.maximum(total, 1e-30))
                stepped = src[h, at(z, r), :] + rate_of[h, at(z, r), :] * ((1.0 / 6.0) * norm - 1.0)
                put(h, zi, t, r, combine(h, z, r, stepped))

    return plane


def y_pass(count, plane):
    def two_planes(i, carry):
        plane(2 * i, 0)
        plane(2 * i + 1, 1)
        return carry

    lax.fori_loop(0, count // 2, two_planes, 0)


def x_parts(load, side, acc, scr, z0, acc0, r0, tile_list, fresh):
    lane = lax.broadcasted_iota(jnp.int32, (8, 128), 1)
    below_last = lane < 127
    below_two = lane < 126
    above_first = lane > 0
    shifted, finished = scr

    def shift(z, s):
        for t in tile_list:
            even, odd = load(0, z, r0 + 8 * t), load(1, z, r0 + 8 * t)
            rows = pl.ds(8 * t, 8)
            shifted[s, 0, rows, :] = jnp.where(above_first, pltpu.roll(even, 1, 1), even)
            shifted[s, 1, rows, :] = jnp.where(above_first, pltpu.roll(odd, 1, 1), even)
            shifted[s, 2, rows, :] = jnp.where(below_last, pltpu.roll(even, 127, 1), odd)
            odd_up = jnp.where(below_last, pltpu.roll(odd, 127, 1), odd)
            shifted[s, 3, rows, :] = odd_up
            shifted[s, 4, rows, :] = jnp.where(below_two, pltpu.roll(even, 126, 1), odd_up)

    def put(h, k, t, back, fore):
        wind = side[h, at(z0 + k, r0 + 8 * t), :]
        rows = pl.ds((acc0 + k) * 48 + 8 * t, 8)
        share = upwind(back, fore, wind)
        acc[h, rows, :] = share if fresh else acc[h, rows, :] + share

    def finish_even(k, s):
        for t in tile_list:
            rows = pl.ds(8 * t, 8)
            put(0, k, t, finished[s, 0, rows, :], finished[s, 1, rows, :])

    def faces(k, s):
        z = z0 + k
        for t in tile_list:
            rows = pl.ds(8 * t, 8)
            u = [
                shifted[s, 0, rows, :],
                shifted[s, 1, rows, :],
                load(0, z, r0 + 8 * t),
                load(1, z, r0 + 8 * t),
                shifted[s, 2, rows, :],
                shifted[s, 3, rows, :],
                shifted[s, 4, rows, :],
            ]
            d = [u[i + 1] - u[i] for i in range(6)]
            e = [d[i + 1] - d[i] for i in range(5)]
            c = [e[i + 1] - e[i] for i in range(4)]
            jump = [c[i + 1] - c[i] for i in range(3)]
            tri = [triple(e[i], e[i + 1], c[i]) for i in range(4)]
            back_even, fore_even = face(
                tri[0][0], tri[1][1], tri[2][2], jump[0], jump[1], *bases(d[2], e[1], e[2])
            )
            back_odd, fore_odd = face(
                tri[1][0], tri[2][1], tri[3][2], jump[1], jump[2], *bases(d[3], e[2], e[3])
            )
            p = tri[0][1] * tri[1][2]
            r = (1.5 * EPS * EPS) * tri[0][1]
            edge = (e[1] + e[1]) - (p * c[0] + r * jump[0]) / (
                (0.5 * p + r) + (3.0 * EPS * EPS) * tri[1][2]
            )
            finished[s, 0, rows, :] = jnp.where(above_first, pltpu.roll(back_odd, 1, 1), edge)
            finished[s, 1, rows, :] = fore_even
            put(1, k, t, back_even, fore_odd)

    return lambda k, s: shift(z0 + k, s), finish_even, faces


def x_pass(load, side, acc, scr, z0, count, acc0, r0, tile_list):
    shift, finish_even, faces = x_parts(load, side, acc, scr, z0, acc0, r0, tile_list, True)
    shift(0, 0)

    def planes(i, carry):
        for s in range(2):
            k = 2 * i + s
            shift(k + 1, (s + 1) % 2)
            finish_even(jnp.maximum(k - 1, 0) if s == 0 else k - 1, (s - 1) % 2)
            faces(k, s)
        return carry

    lax.fori_loop(0, count // 2, planes, 0)
    finish_even(count - 1, 1)


def xy_pass(load, side, acc, scr, z0, count, r0, tile_list, plane, after=None, tail=None):
    shift, finish_even, faces = x_parts(load, side, acc, scr, z0, 0, r0, tile_list, False)
    shift(0, 0)
    shift(1, 1)
    faces(0, 0)
    shift(2, 0)
    finish_even(0, 0)
    faces(1, 1)

    def planes(i, carry):
        for s in range(2):
            k = 2 * i + s
            shift(k + 1, (s + 1) % 2)
            finish_even(k - 1, (s - 1) % 2)
            faces(k, s)
            plane(k - 2, s)
            if after is not None:
                after(jnp.maximum(k - 4, 0))
        return carry

    lax.fori_loop(1, count // 2, planes, 0)
    if after is not None:
        tail()
        after(count - 4)
        after(count - 3)
    finish_even(count - 1, 1)
    plane(count - 2, 0)
    plane(count - 1, 1)
    if after is not None:
        after(count - 2)
        after(count - 1)


def from_work(work):
    return lambda h, z, r: work[h, at(z, r), :]


def position():
    gz, gy = lax.axis_index("gz"), lax.axis_index("gy")
    return lax.rem(gz, 2), lax.rem(gy, 2), gy == 0, gy == lax.axis_size("gy") - 1


def load_planes(work, ref, start, count):
    def one(k, carry):
        for t in range(4):
            for h in range(2):
                work[h, at(start + k, ROW0 + 8 * t), :] = ref[k, h, 8 * t : 8 * t + 8, :]
        return carry

    lax.fori_loop(0, count, one, 0)


NINTH, NEXT, FAR, SLAB = 128, 144, 192, 216


def slab_planes():
    near = [(DEEP - 3 + i if i < 3 else DEEP + 13 + i, NEXT + 8 * i, 8) for i in range(6)]
    far = [(DEEP - 6 + i if i < 3 else DEEP + 16 + i, FAR + 4 * i, 4) for i in range(6)]
    return near + far


def load_rows(work, yo_ref, ye_ref, odd_y):
    def both(low, high):
        def own(i, carry):
            for sub in range(2):
                k = 2 * i + sub
                z = DEEP + k
                for h in range(2):
                    work[h, at(z, ROW0 - 8), :] = low[h, pl.ds(8 * k, 8), :]
                    work[h, at(z, ROW0 - 9, 1), :] = low[h, pl.ds(NINTH + k, 1), :]
                    work[h, at(z, ROW0 + 32), :] = high[h, pl.ds(8 * k, 8), :]
                    work[h, at(z, ROW0 + 40, 1), :] = high[h, pl.ds(NINTH + k, 1), :]
            return carry

        lax.fori_loop(0, 8, own, 0)
        for z, row, n in slab_planes():
            for h in range(2):
                work[h, at(z, ROW0 - n, n), :] = low[h, row : row + n, :]
                work[h, at(z, ROW0 + 32, n), :] = high[h, row : row + n, :]

    @pl.when(odd_y == 0)
    def _():
        both(yo_ref, ye_ref)

    @pl.when(odd_y == 1)
    def _():
        both(ye_ref, yo_ref)


def signs(load, weight, side, z0, count, row_list):
    def one(k, carry):
        z = z0 + k
        for h in range(2):
            for r in row_list:
                v = load(h, z, r)
                weight[h, at(z, r), :] = (-TAU) * (v * lax.rsqrt(v * v + 1.0))
                side[h, at(z, r), :] = jnp.where(v >= 0.0, 1.0, -1.0)
        return carry

    lax.fori_loop(0, count, one, 0)


def edge_rows(work, start, count, far, is_first, is_last):
    @pl.when(is_first)
    def _():
        def one(k, carry):
            z = start + k
            for h in range(2):
                row = work[h, at(z, ROW0, 1), :]
                work[h, at(z, ROW0 - 8), :] = jnp.broadcast_to(row, (8, 128))
                if far:
                    work[h, at(z, ROW0 - 9, 1), :] = row
            return carry

        lax.fori_loop(0, count, one, 0)

    @pl.when(is_last)
    def _():
        def one(k, carry):
            z = start + k
            for h in range(2):
                row = work[h, at(z, ROW0 + 31, 1), :]
                work[h, at(z, ROW0 + 32), :] = jnp.broadcast_to(row, (8, 128))
                if far:
                    work[h, at(z, ROW0 + 40, 1), :] = row
            return carry

        lax.fori_loop(0, count, one, 0)


OWN_ROWS = tuple(ROW0 + 8 * t for t in range(4))
WIDE = ROW0 - 8
OWN_TILES = (1, 2, 3, 4)


def own_kernel(initial, own_ref, *refs):
    if initial:
        weight, side, acc, shifted, finished = refs

        def load(h, z, r):
            return own_ref[z - DEEP, h, pl.ds(r - ROW0, 8), :]

        signs(load, weight, side, DEEP, 16, OWN_ROWS)
    else:
        side, acc, shifted, finished = refs

    def load_clamped(h, z, r):
        return own_ref[jnp.minimum(z - DEEP, 15), h, pl.ds(r - ROW0, 8), :]

    x_pass(load_clamped, side, acc, (shifted, finished), DEEP, 16, 6, WIDE, OWN_TILES)


def planes_kernel(initial, own_ref, zo_ref, ze_ref, *refs):
    if initial:
        _, _, _, weight, side, acc, u, shifted, finished = refs
    else:
        side, _, acc, u, shifted, finished = refs
    odd_z, _, _, _ = position()
    load_planes(u, own_ref, DEEP, 16)
    load_planes(u, zo_ref, 25 * odd_z, DEEP)
    load_planes(u, ze_ref, 25 * (1 - odd_z), DEEP)
    load = from_work(u)
    for z0 in (3, 25):
        if initial:
            signs(load, weight, side, z0, 6, OWN_ROWS)
        x_pass(load, side, acc, (shifted, finished), z0, 6, z0 - 3, WIDE, OWN_TILES)
    z_pass(u, side, acc, 6, WIDE, 4, 1)


def rest_kernel(initial, yo_ref, ye_ref, *refs):
    refs = list(refs)
    if initial:
        out_ref, so_ref, se_ref, weight, side, acc, u = refs[4:11]
        refs = refs[11:]
    else:
        weight, side = refs[:2]
        out_ref, acc, u = refs[4:7]
        refs = refs[7:]
    first, second = refs[:2]
    scr = refs[2:9]
    x_scr = refs[9:11]
    third = refs[11]
    if not initial:
        merged, sems = refs[12:14]
    odd_z, odd_y, is_first, is_last = position()
    load_rows(u, yo_ref, ye_ref, odd_y)
    edge_rows(u, 0, 34, True, is_first, is_last)
    if initial:
        signs(from_work(u), weight, side, 6, 22, (WIDE, WIDE + 40))

    def store(work, start):
        def put(h, zi, t, r, value):
            work[h, at(start + zi, r), :] = value

        return put

    def put_out(h, zi, t, r, value):
        out_ref[zi, h, 8 * t : 8 * t + 8, :] = value

    def put_third(h, zi, t, r, value):
        third[h, pl.ds(zi * 32 + 8 * t, 8), :] = value

    def second_stage(h, z, r, v):
        return 0.75 * u[h, at(z, r), :] + 0.25 * v

    def third_stage(h, z, r, v):
        return (1.0 / 3.0) * u[h, at(z, r), :] + (2.0 / 3.0) * v

    z_pass(u, side, acc, 3, WIDE, 2, 0, 5, 3, True)
    rows = (1, 9, 17, 25, 33, 41)
    rows = rows, rows, rows + (42,)
    plane = y_plane(u, side, weight, acc, scr, store(first, 3), lambda h, z, r, v: v, 6, WIDE, 6, 6, rows)
    xy_pass(from_work(u), side, acc, x_scr, 3, 28, WIDE, (0, 5), plane)
    edge_rows(first, 3, 28, False, is_first, is_last)
    z_pass(first, side, acc, 3, ROW0 - 3, 5, fresh=True)
    rows = tuple(range(0, 48, 8))
    below = tuple(range(-1, 47, 8))
    plane = y_plane(
        first, side, weight, acc, scr, store(second, 6), second_stage, 3, ROW0 - 3, 5, 5, (rows, below, below)
    )
    xy_pass(from_work(first), side, acc, x_scr, 6, 22, ROW0 - 3, range(5), plane)
    edge_rows(second, 6, 22, False, is_first, is_last)
    z_pass(second, side, acc, 0, ROW0, 4, fresh=True)
    put = put_out if initial else put_third
    rows, below = rows[:5], below[:5]
    plane = y_plane(second, side, weight, acc, scr, put, third_stage, 0, ROW0, 4, 5, (rows, below, below))

    if initial:
        xy_pass(from_work(second), side, acc, x_scr, 9, 16, ROW0, range(4), plane)

        def slabs(k, carry):
            so_ref[k] = out_ref[k + 7 * odd_z]
            se_ref[k] = out_ref[k + 7 * (1 - odd_z)]
            return carry

        lax.fori_loop(0, DEEP, slabs, 0)
    else:
        lane = lax.broadcasted_iota(jnp.int32, (8, 128), 1)
        even = (lane & 1) == 0
        half = lane >> 1

        def merge(k):
            for t in range(4):
                rows = pl.ds(k * 32 + 8 * t, 8)
                for h in range(2):
                    parts = [jnp.take_along_axis(third[p, rows, :], half + 64 * h, axis=1) for p in range(2)]
                    merged[k, 8 * t : 8 * t + 8, 128 * h : 128 * h + 128] = jnp.where(even, *parts)

        copies = []
        for chunk in range(4):
            planes = pl.ds(4 * chunk, 4)
            copies.append(pltpu.make_async_copy(merged.at[planes], out_ref.at[planes], sems.at[chunk]))

        def tail():
            for copy in copies[:3]:
                copy.start()

        xy_pass(from_work(second), side, acc, x_scr, 9, 16, ROW0, range(4), plane, merge, tail)
        copies[3].start()
        for copy in copies:
            copy.wait()


def split_kernel(own_ref, out_ref, so_ref, se_ref):
    odd_z = lax.rem(lax.axis_index("gz"), 2)
    lane = lax.broadcasted_iota(jnp.int32, (8, 128), 1)
    low = lane < 64
    twice = (lane & 63) * 2
    for chunk in range(4):
        for k in range(4 * chunk, 4 * chunk + 4):
            for t in range(4):
                v = [own_ref[k, 8 * t : 8 * t + 8, 128 * h : 128 * h + 128] for h in range(2)]
                for p in range(2):
                    parts = [jnp.take_along_axis(x, twice + p, axis=1) for x in v]
                    out_ref[k, p, 8 * t : 8 * t + 8, :] = jnp.where(low, *parts)

    def slabs(k, carry):
        so_ref[k] = out_ref[k + 7 * odd_z]
        se_ref[k] = out_ref[k + 7 * (1 - odd_z)]
        return carry

    lax.fori_loop(0, DEEP, slabs, 0)


def pack_kernel(own_ref, zo_ref, ze_ref, yo_ref, ye_ref):
    odd_z, odd_y, _, _ = position()

    def fill(out, top, low_ref, high_ref):
        main, ninth, short = (24, 23, 28) if top else (0, 8, 0)

        def own(i, carry):
            for sub in range(2):
                k = 2 * i + sub
                for h in range(2):
                    out[h, pl.ds(8 * k, 8), :] = own_ref[k, h, main : main + 8, :]
                    out[h, pl.ds(NINTH + k, 1), :] = own_ref[k, h, ninth : ninth + 1, :]
            return carry

        lax.fori_loop(0, 8, own, 0)
        for z, row, n in slab_planes():
            ref, k = (low_ref, z) if z < DEEP else (high_ref, z - DEEP - 16)
            first = main if n == 8 else short
            for h in range(2):
                out[h, row : row + n, :] = ref[k, h, first : first + n, :]

    for z_parity in range(2):
        for y_parity in range(2):

            @pl.when((odd_z == z_parity) & (odd_y == y_parity))
            def _(z_parity=z_parity, y_parity=y_parity):
                low_ref, high_ref = (ze_ref, zo_ref) if z_parity else (zo_ref, ze_ref)
                fill(yo_ref, y_parity == 1, low_ref, high_ref)
                fill(ye_ref, y_parity == 0, low_ref, high_ref)


def swaps(count, start, periodic):
    pairs = []
    for low in range(start, count, 2):
        if low + 1 < count or periodic:
            high = (low + 1) % count
            pairs += [(low, high), (high, low)]
    return pairs


VMEM = pl.BlockSpec(memory_space=pltpu.VMEM)
WORK = (2, 34 * PITCH, 128)
ACC = (2, 28 * 48, 128)


def call(kernel, name, args, outs, scratch=(), aliases=None, cycles=1000, hbm=()):
    anywhere = pl.BlockSpec(memory_space=pltpu.HBM)
    more = [pltpu.VMEM((16, 32, 256), f32), pltpu.SemaphoreType.DMA((4,))] if hbm else []
    return pl.pallas_call(
        kernel,
        out_shape=[jax.ShapeDtypeStruct(shape, f32) for shape in outs],
        in_specs=[anywhere if ("in", i) == hbm else VMEM for i in range(len(args))],
        out_specs=[anywhere if ("out", i) == hbm else VMEM for i in range(len(outs))],
        scratch_shapes=[pltpu.VMEM(shape, f32) for shape in scratch] + more,
        input_output_aliases=aliases or {},
        compiler_params=pltpu.CompilerParams(vmem_limit_bytes=24 * 1024 * 1024),
        cost_estimate=pl.CostEstimate(flops=4096 * cycles, bytes_accessed=4096 * cycles, transcendentals=0),
        name=name,
    )(*args)


def per_device(level_set):
    n_z, n_y = lax.axis_size("gz"), lax.axis_size("gy")
    z_odd, z_even = swaps(n_z, 1, True), swaps(n_z, 0, True)
    y_odd, y_even = swaps(n_y, 1, False), swaps(n_y, 0, False)
    split, deep, slab = (16, 2, 32, 128), (DEEP, 2, 32, 128), (2, SLAB, 128)
    shifts = [(2, 5, 48, 128), (2, 2, 48, 128)]
    rest_scratch = [WORK] * 2 + [(4, 56, 128)] * 7 + shifts + [(2, 512, 128)]
    field, z_send_odd, z_send_even = call(split_kernel, "split_cells", (level_set,), [split, deep, deep])
    weight = side = None
    for step in range(STEPS):
        initial = step == 0
        zo = lax.ppermute(z_send_odd, "gz", z_odd)
        ze = lax.ppermute(z_send_even, "gz", z_even)
        own = functools.partial(own_kernel, initial)
        planes = functools.partial(planes_kernel, initial)
        rest = functools.partial(rest_kernel, initial)
        if initial:
            weight, side, acc = call(own, "own_planes", (field,), [WORK, WORK, ACC], shifts, cycles=4000)
        else:
            (acc,) = call(own, "own_planes_next", (field, side), [ACC], shifts, cycles=4000)
        y_send_odd, y_send_even = call(pack_kernel, "pack_rows", (field, zo, ze), [slab, slab])
        yo = lax.ppermute(y_send_odd, "gy", y_odd)
        ye = lax.ppermute(y_send_even, "gy", y_even)
        if initial:
            weight, side, acc, u = call(
                planes,
                "ghost_planes",
                (field, zo, ze, weight, side, acc),
                [WORK, WORK, ACC, WORK],
                shifts,
                {3: 0, 4: 1, 5: 2},
                8000,
            )
            field, z_send_odd, z_send_even, weight, side, _, _ = call(
                rest,
                "first_step",
                (yo, ye, weight, side, acc, u),
                [split, deep, deep, WORK, WORK, ACC, WORK],
                rest_scratch,
                {2: 3, 3: 4, 4: 5, 5: 6},
                30000,
            )
        else:
            acc, u = call(
                planes,
                "ghost_planes_next",
                (field, zo, ze, side, acc),
                [ACC, WORK],
                shifts,
                {4: 0},
                8000,
            )
            field, _, _ = call(
                rest,
                "next_step",
                (yo, ye, weight, side, acc, u),
                [(16, 32, 256), ACC, WORK],
                rest_scratch,
                {4: 1, 5: 2},
                30000,
                ("out", 0),
            )
    return field


def solution(mesh):
    return jax.shard_map(
        per_device,
        mesh=mesh,
        in_specs=(P("gz", "gy", None),),
        out_specs=P("gz", "gy", None),
        check_vma=False,
    )
```

```python
import functools

import jax
import jax.numpy as jnp
from jax import lax
from jax.experimental import pallas as pl
from jax.experimental.pallas import tpu as pltpu
from jax.sharding import PartitionSpec as P

STEPS = 2
TAU = 0.3
EPS = 0.75e-6

DEEP = 9
PITCH = 64
ROW0 = 16
f32 = jnp.float32


def triple(g, h, curve):
    lean = 1.5 * curve
    mid = curve * curve + (0.75 * (g * h) + EPS)
    left = mid + lean * h
    right = mid - lean * g
    return left * left, mid * mid, right * right


def face(a, b, c, jump_low, jump_high, base_back, base_fore):
    p = b * c
    q = a * c
    r = a * b
    half = 0.5 * (p + r) + 3.0 * q
    pj = p * jump_low
    rj = r * jump_high
    back = base_back - (pj + 1.5 * rj) / (half + r)
    fore = base_fore - (1.5 * pj + rj) / (half + p)
    return back, fore


def upwind(back, fore, side):
    best = jnp.maximum(jnp.maximum(side * back, side * fore), 0.0)
    return best * best


def bases(center, low_slope, high_slope):
    six = 6.0 * center
    both = low_slope + high_slope
    return six + (both + high_slope), (both + low_slope) - six


def at(z, r, n=8):
    return pl.ds(z * PITCH + r, n)


def z_pass(src, side, acc, margin, r0, tiles, first_tile=0, tile_step=1, acc0=0, fresh=False):
    first = DEEP - margin
    last = DEEP + 16 + margin

    def column(i, carry):
        t = first_tile + tile_step * i
        r = r0 + 8 * t
        state = [dict(), dict()]
        for k in range(first - 1, last):
            for h in range(2):
                s = state[h]

                def u(z):
                    if ("u", z) not in s:
                        s["u", z] = src[h, at(z, r), :]
                    return s["u", z]

                def d(z):
                    if ("d", z) not in s:
                        s["d", z] = u(z + 1) - u(z)
                    return s["d", z]

                def e(z):
                    if ("e", z) not in s:
                        s["e", z] = d(z + 1) - d(z)
                    return s["e", z]

                def c(z):
                    if ("c", z) not in s:
                        s["c", z] = e(z) - e(z - 1)
                    return s["c", z]

                def j(z):
                    if ("j", z) not in s:
                        s["j", z] = c(z) - c(z - 1)
                    return s["j", z]

                def tr(z):
                    if ("t", z) not in s:
                        s["t", z] = triple(e(z - 1), e(z), c(z))
                    return s["t", z]

                base_back, base_fore = bases(d(k), e(k - 1), e(k))
                back, fore = face(
                    tr(k - 1)[0], tr(k)[1], tr(k + 1)[2], j(k), j(k + 1), base_back, base_fore
                )
                if k >= first:
                    rows = pl.ds((acc0 + k - first) * 48 + 8 * t, 8)
                    share = upwind(s["back"], fore, side[h, at(k, r), :])
                    acc[h, rows, :] = share if fresh else acc[h, rows, :] + share
                s["back"] = back
        return carry

    lax.fori_loop(0, tiles, column, 0)


def y_plane(src, side, rate_of, acc, scr, put, combine, margin, r0, tiles, face_tiles, rows):
    first = DEEP - margin
    left_s, mid_s, right_s, curve_s, diff_s, slope_s, fore_s = scr
    triple_rows, slope_rows, diff_rows = rows

    def plane(zi, sub):
        z = first + zi
        for h in range(2):
            slot = sub * 2 + h
            for row in diff_rows:
                r = r0 - 2 + row
                diff_s[slot, pl.ds(row + 1, 8), :] = src[h, at(z, r + 1), :] - src[h, at(z, r), :]
            for row in slope_rows:
                above, below = diff_s[slot, pl.ds(row + 2, 8), :], diff_s[slot, pl.ds(row + 1, 8), :]
                slope_s[slot, pl.ds(row + 1, 8), :] = above - below
            for row in triple_rows:
                g, e = slope_s[slot, pl.ds(row, 8), :], slope_s[slot, pl.ds(row + 1, 8), :]
                curve = e - g
                rows = pl.ds(row, 8)
                left_s[slot, rows, :], mid_s[slot, rows, :], right_s[slot, rows, :] = triple(g, e, curve)
                curve_s[slot, rows, :] = curve
        for h in range(2):
            slot = sub * 2 + h
            backs = []
            for t in range(face_tiles):
                lo, me, hi = pl.ds(8 * t, 8), pl.ds(8 * t + 1, 8), pl.ds(8 * t + 2, 8)
                cm = curve_s[slot, me, :]
                back, fore = face(
                    left_s[slot, lo, :],
                    mid_s[slot, me, :],
                    right_s[slot, hi, :],
                    cm - curve_s[slot, lo, :],
                    curve_s[slot, hi, :] - cm,
                    *bases(diff_s[slot, hi, :], slope_s[slot, me, :], slope_s[slot, hi, :]),
                )
                fore_s[slot, pl.ds(8 * t, 8), :] = fore
                backs.append(back)
            for t in range(tiles):
                r = r0 + 8 * t
                fore = fore_s[slot, pl.ds(8 * t + 1, 8), :]
                total = acc[h, pl.ds(zi * 48 + 8 * t, 8), :] + upwind(
                    backs[t], fore, side[h, at(z, r), :]
                )
                norm = total * lax.rsqrt(jnp.maximum(total, 1e-30))
                stepped = src[h, at(z, r), :] + rate_of[h, at(z, r), :] * ((1.0 / 6.0) * norm - 1.0)
                put(h, zi, t, r, combine(h, z, r, stepped))

    return plane


def y_pass(count, plane):
    def two_planes(i, carry):
        plane(2 * i, 0)
        plane(2 * i + 1, 1)
        return carry

    lax.fori_loop(0, count // 2, two_planes, 0)


def x_parts(load, side, acc, scr, z0, acc0, r0, tile_list, fresh):
    lane = lax.broadcasted_iota(jnp.int32, (8, 128), 1)
    below_last = lane < 127
    below_two = lane < 126
    above_first = lane > 0
    shifted, finished = scr

    def shift(z, s):
        for t in tile_list:
            even, odd = load(0, z, r0 + 8 * t), load(1, z, r0 + 8 * t)
            rows = pl.ds(8 * t, 8)
            shifted[s, 0, rows, :] = jnp.where(above_first, pltpu.roll(even, 1, 1), even)
            shifted[s, 1, rows, :] = jnp.where(above_first, pltpu.roll(odd, 1, 1), even)
            shifted[s, 2, rows, :] = jnp.where(below_last, pltpu.roll(even, 127, 1), odd)
            odd_up = jnp.where(below_last, pltpu.roll(odd, 127, 1), odd)
            shifted[s, 3, rows, :] = odd_up
            shifted[s, 4, rows, :] = jnp.where(below_two, pltpu.roll(even, 126, 1), odd_up)

    def put(h, k, t, back, fore):
        wind = side[h, at(z0 + k, r0 + 8 * t), :]
        rows = pl.ds((acc0 + k) * 48 + 8 * t, 8)
        share = upwind(back, fore, wind)
        acc[h, rows, :] = share if fresh else acc[h, rows, :] + share

    def finish_even(k, s):
        for t in tile_list:
            rows = pl.ds(8 * t, 8)
            put(0, k, t, finished[s, 0, rows, :], finished[s, 1, rows, :])

    def faces(k, s):
        z = z0 + k
        for t in tile_list:
            rows = pl.ds(8 * t, 8)
            u = [
                shifted[s, 0, rows, :],
                shifted[s, 1, rows, :],
                load(0, z, r0 + 8 * t),
                load(1, z, r0 + 8 * t),
                shifted[s, 2, rows, :],
                shifted[s, 3, rows, :],
                shifted[s, 4, rows, :],
            ]
            d = [u[i + 1] - u[i] for i in range(6)]
            e = [d[i + 1] - d[i] for i in range(5)]
            c = [e[i + 1] - e[i] for i in range(4)]
            jump = [c[i + 1] - c[i] for i in range(3)]
            tri = [triple(e[i], e[i + 1], c[i]) for i in range(4)]
            back_even, fore_even = face(
                tri[0][0], tri[1][1], tri[2][2], jump[0], jump[1], *bases(d[2], e[1], e[2])
            )
            back_odd, fore_odd = face(
                tri[1][0], tri[2][1], tri[3][2], jump[1], jump[2], *bases(d[3], e[2], e[3])
            )
            p = tri[0][1] * tri[1][2]
            r = (1.5 * EPS * EPS) * tri[0][1]
            edge = (e[1] + e[1]) - (p * c[0] + r * jump[0]) / (
                (0.5 * p + r) + (3.0 * EPS * EPS) * tri[1][2]
            )
            finished[s, 0, rows, :] = jnp.where(above_first, pltpu.roll(back_odd, 1, 1), edge)
            finished[s, 1, rows, :] = fore_even
            put(1, k, t, back_even, fore_odd)

    return lambda k, s: shift(z0 + k, s), finish_even, faces


def x_pass(load, side, acc, scr, z0, count, acc0, r0, tile_list):
    shift, finish_even, faces = x_parts(load, side, acc, scr, z0, acc0, r0, tile_list, True)
    shift(0, 0)

    def planes(i, carry):
        for s in range(2):
            k = 2 * i + s
            shift(k + 1, (s + 1) % 2)
            finish_even(jnp.maximum(k - 1, 0) if s == 0 else k - 1, (s - 1) % 2)
            faces(k, s)
        return carry

    lax.fori_loop(0, count // 2, planes, 0)
    finish_even(count - 1, 1)


def xy_pass(load, side, acc, scr, z0, count, r0, tile_list, plane, after=None, tail=None):
    shift, finish_even, faces = x_parts(load, side, acc, scr, z0, 0, r0, tile_list, False)
    shift(0, 0)
    shift(1, 1)
    faces(0, 0)
    shift(2, 0)
    finish_even(0, 0)
    faces(1, 1)

    def planes(i, carry):
        for s in range(2):
            k = 2 * i + s
            shift(k + 1, (s + 1) % 2)
            finish_even(k - 1, (s - 1) % 2)
            faces(k, s)
            plane(k - 2, s)
            if after is not None:
                after(jnp.maximum(k - 4, 0))
        return carry

    lax.fori_loop(1, count // 2, planes, 0)
    if after is not None:
        tail()
        after(count - 4)
        after(count - 3)
    finish_even(count - 1, 1)
    plane(count - 2, 0)
    plane(count - 1, 1)
    if after is not None:
        after(count - 2)
        after(count - 1)


def from_work(work):
    return lambda h, z, r: work[h, at(z, r), :]


def position():
    gz, gy = lax.axis_index("gz"), lax.axis_index("gy")
    return lax.rem(gz, 2), lax.rem(gy, 2), gy == 0, gy == lax.axis_size("gy") - 1


def load_planes(work, ref, start, count):
    step = 4 if count % 4 == 0 else 3

    def some(i, carry):
        for k in (step * i + sub for sub in range(step)):
            for t in range(4):
                for h in range(2):
                    work[h, at(start + k, ROW0 + 8 * t), :] = ref[k, h, 8 * t : 8 * t + 8, :]
        return carry

    lax.fori_loop(0, count // step, some, 0)


NINTH, NEXT, FAR, SLAB = 128, 144, 192, 216


def slab_planes():
    near = [(DEEP - 3 + i if i < 3 else DEEP + 13 + i, NEXT + 8 * i, 8) for i in range(6)]
    far = [(DEEP - 6 + i if i < 3 else DEEP + 16 + i, FAR + 4 * i, 4) for i in range(6)]
    return near + far


def load_rows(work, yo_ref, ye_ref, odd_y):
    def both(low, high):
        def own(i, carry):
            for sub in range(2):
                k = 2 * i + sub
                z = DEEP + k
                for h in range(2):
                    work[h, at(z, ROW0 - 8), :] = low[h, pl.ds(8 * k, 8), :]
                    work[h, at(z, ROW0 - 9, 1), :] = low[h, pl.ds(NINTH + k, 1), :]
                    work[h, at(z, ROW0 + 32), :] = high[h, pl.ds(8 * k, 8), :]
                    work[h, at(z, ROW0 + 40, 1), :] = high[h, pl.ds(NINTH + k, 1), :]
            return carry

        lax.fori_loop(0, 8, own, 0)
        for z, row, n in slab_planes():
            for h in range(2):
                work[h, at(z, ROW0 - n, n), :] = low[h, row : row + n, :]
                work[h, at(z, ROW0 + 32, n), :] = high[h, row : row + n, :]

    @pl.when(odd_y == 0)
    def _():
        both(yo_ref, ye_ref)

    @pl.when(odd_y == 1)
    def _():
        both(ye_ref, yo_ref)


def signs(load, weight, side, z0, count, row_list):
    def two(i, carry):
        for z in (z0 + 2 * i, z0 + 2 * i + 1):
            for h in range(2):
                for r in row_list:
                    v = load(h, z, r)
                    weight[h, at(z, r), :] = (-TAU) * (v * lax.rsqrt(v * v + 1.0))
                    side[h, at(z, r), :] = jnp.where(v >= 0.0, 1.0, -1.0)
        return carry

    lax.fori_loop(0, count // 2, two, 0)


def edge_rows(work, start, count, far, is_first, is_last):
    @pl.when(is_first)
    def _():
        def one(k, carry):
            z = start + k
            for h in range(2):
                row = work[h, at(z, ROW0, 1), :]
                work[h, at(z, ROW0 - 8), :] = jnp.broadcast_to(row, (8, 128))
                if far:
                    work[h, at(z, ROW0 - 9, 1), :] = row
            return carry

        lax.fori_loop(0, count, one, 0)

    @pl.when(is_last)
    def _():
        def one(k, carry):
            z = start + k
            for h in range(2):
                row = work[h, at(z, ROW0 + 31, 1), :]
                work[h, at(z, ROW0 + 32), :] = jnp.broadcast_to(row, (8, 128))
                if far:
                    work[h, at(z, ROW0 + 40, 1), :] = row
            return carry

        lax.fori_loop(0, count, one, 0)


OWN_ROWS = tuple(ROW0 + 8 * t for t in range(4))
WIDE = ROW0 - 8
OWN_TILES = (1, 2, 3, 4)


def own_kernel(initial, own_ref, *refs):
    if initial:
        weight, side, acc, shifted, finished = refs

        def load(h, z, r):
            return own_ref[z - DEEP, h, pl.ds(r - ROW0, 8), :]

        signs(load, weight, side, DEEP, 16, OWN_ROWS)
    else:
        side, acc, shifted, finished = refs

    def load_clamped(h, z, r):
        return own_ref[jnp.minimum(z - DEEP, 15), h, pl.ds(r - ROW0, 8), :]

    x_pass(load_clamped, side, acc, (shifted, finished), DEEP, 16, 6, WIDE, OWN_TILES)


def planes_kernel(initial, own_ref, zo_ref, ze_ref, *refs):
    if initial:
        _, _, _, weight, side, acc, u, shifted, finished = refs
    else:
        side, _, acc, u, shifted, finished = refs
    odd_z, _, _, _ = position()
    load_planes(u, own_ref, DEEP, 16)
    load_planes(u, zo_ref, 25 * odd_z, DEEP)
    load_planes(u, ze_ref, 25 * (1 - odd_z), DEEP)
    load = from_work(u)
    for z0 in (3, 25):
        if initial:
            signs(load, weight, side, z0, 6, OWN_ROWS)
        x_pass(load, side, acc, (shifted, finished), z0, 6, z0 - 3, WIDE, OWN_TILES)
    z_pass(u, side, acc, 6, WIDE, 4, 1)


def rest_kernel(initial, yo_ref, ye_ref, *refs):
    refs = list(refs)
    if initial:
        out_ref, so_ref, se_ref, weight, side, acc, u = refs[4:11]
        refs = refs[11:]
    else:
        weight, side = refs[:2]
        out_ref, acc, u = refs[4:7]
        refs = refs[7:]
    first, second = refs[:2]
    scr = refs[2:9]
    x_scr = refs[9:11]
    third = refs[11]
    if not initial:
        merged, sems = refs[12:14]
    odd_z, odd_y, is_first, is_last = position()
    load_rows(u, yo_ref, ye_ref, odd_y)
    edge_rows(u, 0, 34, True, is_first, is_last)
    if initial:
        signs(from_work(u), weight, side, 6, 22, (WIDE, WIDE + 40))

    def store(work, start):
        def put(h, zi, t, r, value):
            work[h, at(start + zi, r), :] = value

        return put

    def put_out(h, zi, t, r, value):
        out_ref[zi, h, 8 * t : 8 * t + 8, :] = value

    def put_third(h, zi, t, r, value):
        third[h, pl.ds(zi * 32 + 8 * t, 8), :] = value

    def second_stage(h, z, r, v):
        return 0.75 * u[h, at(z, r), :] + 0.25 * v

    def third_stage(h, z, r, v):
        return (1.0 / 3.0) * u[h, at(z, r), :] + (2.0 / 3.0) * v

    z_pass(u, side, acc, 3, WIDE, 2, 0, 5, 3, True)
    rows = (1, 9, 17, 25, 33, 41)
    rows = rows, rows, rows + (42,)
    plane = y_plane(u, side, weight, acc, scr, store(first, 3), lambda h, z, r, v: v, 6, WIDE, 6, 6, rows)
    xy_pass(from_work(u), side, acc, x_scr, 3, 28, WIDE, (0, 5), plane)
    edge_rows(first, 3, 28, False, is_first, is_last)
    z_pass(first, side, acc, 3, ROW0 - 3, 5, fresh=True)
    rows = tuple(range(0, 48, 8))
    below = tuple(range(-1, 47, 8))
    plane = y_plane(
        first, side, weight, acc, scr, store(second, 6), second_stage, 3, ROW0 - 3, 5, 5, (rows, below, below)
    )
    xy_pass(from_work(first), side, acc, x_scr, 6, 22, ROW0 - 3, range(5), plane)
    edge_rows(second, 6, 22, False, is_first, is_last)
    z_pass(second, side, acc, 0, ROW0, 4, fresh=True)
    put = put_out if initial else put_third
    rows, below = rows[:5], below[:5]
    plane = y_plane(second, side, weight, acc, scr, put, third_stage, 0, ROW0, 4, 5, (rows, below, below))

    if initial:
        xy_pass(from_work(second), side, acc, x_scr, 9, 16, ROW0, range(4), plane)

        def slabs(k, carry):
            so_ref[k] = out_ref[k + 7 * odd_z]
            se_ref[k] = out_ref[k + 7 * (1 - odd_z)]
            return carry

        lax.fori_loop(0, DEEP, slabs, 0)
    else:
        lane = lax.broadcasted_iota(jnp.int32, (8, 128), 1)
        even = (lane & 1) == 0
        half = lane >> 1

        def merge(k):
            for t in range(4):
                rows = pl.ds(k * 32 + 8 * t, 8)
                for h in range(2):
                    parts = [jnp.take_along_axis(third[p, rows, :], half + 64 * h, axis=1) for p in range(2)]
                    merged[k, 8 * t : 8 * t + 8, 128 * h : 128 * h + 128] = jnp.where(even, *parts)

        copies = []
        for chunk in range(4):
            planes = pl.ds(4 * chunk, 4)
            copies.append(pltpu.make_async_copy(merged.at[planes], out_ref.at[planes], sems.at[chunk]))

        def tail():
            for copy in copies[:3]:
                copy.start()

        xy_pass(from_work(second), side, acc, x_scr, 9, 16, ROW0, range(4), plane, merge, tail)
        copies[3].start()
        for copy in copies:
            copy.wait()


def split_kernel(own_ref, out_ref, so_ref, se_ref):
    odd_z = lax.rem(lax.axis_index("gz"), 2)
    lane = lax.broadcasted_iota(jnp.int32, (8, 128), 1)
    low = lane < 64
    twice = (lane & 63) * 2
    for chunk in range(4):
        for k in range(4 * chunk, 4 * chunk + 4):
            for t in range(4):
                v = [own_ref[k, 8 * t : 8 * t + 8, 128 * h : 128 * h + 128] for h in range(2)]
                for p in range(2):
                    parts = [jnp.take_along_axis(x, twice + p, axis=1) for x in v]
                    out_ref[k, p, 8 * t : 8 * t + 8, :] = jnp.where(low, *parts)

    def slabs(k, carry):
        so_ref[k] = out_ref[k + 7 * odd_z]
        se_ref[k] = out_ref[k + 7 * (1 - odd_z)]
        return carry

    lax.fori_loop(0, DEEP, slabs, 0)


def pack_kernel(own_ref, zo_ref, ze_ref, yo_ref, ye_ref):
    odd_z, odd_y, _, _ = position()

    def fill(out, top, low_ref, high_ref):
        main, ninth, short = (24, 23, 28) if top else (0, 8, 0)

        def own(i, carry):
            for sub in range(2):
                k = 2 * i + sub
                for h in range(2):
                    out[h, pl.ds(8 * k, 8), :] = own_ref[k, h, main : main + 8, :]
                    out[h, pl.ds(NINTH + k, 1), :] = own_ref[k, h, ninth : ninth + 1, :]
            return carry

        lax.fori_loop(0, 8, own, 0)
        for z, row, n in slab_planes():
            ref, k = (low_ref, z) if z < DEEP else (high_ref, z - DEEP - 16)
            first = main if n == 8 else short
            for h in range(2):
                out[h, row : row + n, :] = ref[k, h, first : first + n, :]

    for z_parity in range(2):
        for y_parity in range(2):

            @pl.when((odd_z == z_parity) & (odd_y == y_parity))
            def _(z_parity=z_parity, y_parity=y_parity):
                low_ref, high_ref = (ze_ref, zo_ref) if z_parity else (zo_ref, ze_ref)
                fill(yo_ref, y_parity == 1, low_ref, high_ref)
                fill(ye_ref, y_parity == 0, low_ref, high_ref)


def swaps(count, start, periodic):
    pairs = []
    for low in range(start, count, 2):
        if low + 1 < count or periodic:
            high = (low + 1) % count
            pairs += [(low, high), (high, low)]
    return pairs


VMEM = pl.BlockSpec(memory_space=pltpu.VMEM)
WORK = (2, 34 * PITCH, 128)
ACC = (2, 28 * 48, 128)


def call(kernel, name, args, outs, scratch=(), aliases=None, cycles=1000, hbm=()):
    anywhere = pl.BlockSpec(memory_space=pltpu.HBM)
    more = [pltpu.VMEM((16, 32, 256), f32), pltpu.SemaphoreType.DMA((4,))] if hbm else []
    return pl.pallas_call(
        kernel,
        out_shape=[jax.ShapeDtypeStruct(shape, f32) for shape in outs],
        in_specs=[anywhere if ("in", i) == hbm else VMEM for i in range(len(args))],
        out_specs=[anywhere if ("out", i) == hbm else VMEM for i in range(len(outs))],
        scratch_shapes=[pltpu.VMEM(shape, f32) for shape in scratch] + more,
        input_output_aliases=aliases or {},
        compiler_params=pltpu.CompilerParams(vmem_limit_bytes=24 * 1024 * 1024),
        cost_estimate=pl.CostEstimate(flops=4096 * cycles, bytes_accessed=4096 * cycles, transcendentals=0),
        name=name,
    )(*args)


def per_device(level_set):
    n_z, n_y = lax.axis_size("gz"), lax.axis_size("gy")
    z_odd, z_even = swaps(n_z, 1, True), swaps(n_z, 0, True)
    y_odd, y_even = swaps(n_y, 1, False), swaps(n_y, 0, False)
    split, deep, slab = (16, 2, 32, 128), (DEEP, 2, 32, 128), (2, SLAB, 128)
    shifts = [(2, 5, 48, 128), (2, 2, 48, 128)]
    rest_scratch = [WORK] * 2 + [(4, 56, 128)] * 7 + shifts + [(2, 512, 128)]
    field, z_send_odd, z_send_even = call(split_kernel, "split_cells", (level_set,), [split, deep, deep])
    weight = side = None
    for step in range(STEPS):
        initial = step == 0
        zo = lax.ppermute(z_send_odd, "gz", z_odd)
        ze = lax.ppermute(z_send_even, "gz", z_even)
        own = functools.partial(own_kernel, initial)
        planes = functools.partial(planes_kernel, initial)
        rest = functools.partial(rest_kernel, initial)
        if initial:
            weight, side, acc = call(own, "own_planes", (field,), [WORK, WORK, ACC], shifts, cycles=4000)
        else:
            (acc,) = call(own, "own_planes_next", (field, side), [ACC], shifts, cycles=4000)
        y_send_odd, y_send_even = call(pack_kernel, "pack_rows", (field, zo, ze), [slab, slab])
        yo = lax.ppermute(y_send_odd, "gy", y_odd)
        ye = lax.ppermute(y_send_even, "gy", y_even)
        if initial:
            weight, side, acc, u = call(
                planes,
                "ghost_planes",
                (field, zo, ze, weight, side, acc),
                [WORK, WORK, ACC, WORK],
                shifts,
                {3: 0, 4: 1, 5: 2},
                8000,
            )
            field, z_send_odd, z_send_even, weight, side, _, _ = call(
                rest,
                "first_step",
                (yo, ye, weight, side, acc, u),
                [split, deep, deep, WORK, WORK, ACC, WORK],
                rest_scratch,
                {2: 3, 3: 4, 4: 5, 5: 6},
                30000,
            )
        else:
            acc, u = call(
                planes,
                "ghost_planes_next",
                (field, zo, ze, side, acc),
                [ACC, WORK],
                shifts,
                {4: 0},
                8000,
            )
            field, _, _ = call(
                rest,
                "next_step",
                (yo, ye, weight, side, acc, u),
                [(16, 32, 256), ACC, WORK],
                rest_scratch,
                {4: 1, 5: 2},
                30000,
                ("out", 0),
            )
    return field


def solution(mesh):
    return jax.shard_map(
        per_device,
        mesh=mesh,
        in_specs=(P("gz", "gy", None),),
        out_specs=P("gz", "gy", None),
        check_vma=False,
    )
```
